512 devices in a mesh: grp: 2 (over z_lo), gx: 32 (over y, z_hi), gy: 8 (over x, core).
Axes of the slice: x: 4, y: 8, z: 8 (z_hi: 4, z_lo: 2; z = z_hi * 2 + z_lo), core: 2. Of those that a mesh axis runs over, the one named last changes fastest.
Arguments:
- flow_state: float32 [2, 4, 512, 64, 128], P('grp', None, 'gx', 'gy'), may hold values from -6 to 6
- block_offset: int32 [128], P('gx'), may hold values from -3 to 3, as said below
- block_weight: float32 [128], P('gx'), may hold values from 0.1 to 0.9
Outputs:
- advanced: float32 [2, 4, 512, 64, 128], P('grp', None, 'gx', 'gy')
The draws below stay inside these ranges and needn't reach their ends.
Inputs may be any that keep to these rules, and one draw needn't show every extreme that they name: Block b's lamb reaches blocks b + block_offset[b] and the next one, counted modulo 128; in every brick of 4 blocks the first block has a negative offset and the last block an offset of 0 or more.
All inputs are finite; a program needn't handle non-finite values.
Results may differ from the reference program's by a relative error of at most 0.00005.
Values sent between devices are 32-bit elements; how exact they have to be, the bound alone decides.
A program may use at most 64 MiB of HBM per device.

```python
import jax
import jax.numpy as jnp
from jax import lax

NZ = 128
NB = 4
NX = 512
NY = 64
NBT = 128


def draw_flow_state(key, part):
    return jax.random.truncated_normal(key, -6.0, 6.0, (2, 4, NX, NY, NZ), jnp.float32)


def draw_block_offset(key, part):
    middle = jax.random.randint(jax.random.fold_in(key, 101), (NBT,), 1 - NB, NB, dtype=jnp.int32)
    leading = jax.random.randint(jax.random.fold_in(key, 202), (NBT,), 1 - NB, 0, dtype=jnp.int32)
    trailing = jax.random.randint(jax.random.fold_in(key, 303), (NBT,), 0, NB, dtype=jnp.int32)
    within = jnp.arange(NBT, dtype=jnp.int32) % NB
    chosen = jnp.where(within == 0, leading, middle)
    return jnp.where(within == NB - 1, trailing, chosen).astype(jnp.int32)


def level_of(key, dims, shards, smallest, largest):
    factor_of = 1.0
    for dim, parts in shards:
        draws = jax.random.uniform(jax.random.fold_in(jax.random.fold_in(key, 6), dim), (parts,), jnp.float32, smallest / len(shards), largest / len(shards))
        factor_of = factor_of * jnp.repeat(jnp.exp(draws), dims[dim] // parts).reshape((-1,) + (1,) * (len(dims) - 1 - dim))
    return factor_of


def setup_inputs(seed: int = 0) -> dict:
    arg_keys = jax.random.split(jax.random.key(seed), 4)
    flow_state = draw_flow_state(jax.random.fold_in(arg_keys[3], 71), 0)
    block_offset = draw_block_offset(jax.random.fold_in(arg_keys[3], 71), 0)
    block_weight = jnp.clip(0.1 + 0.79999997 * jax.random.uniform(arg_keys[2], (NBT,), jnp.float32) ** level_of(arg_keys[2], (NBT,), ((0, 32),), -0.2, 0.2), 0.1, 0.9)
    return dict(flow_state=flow_state, block_offset=block_offset, block_weight=block_weight)


drp_weights = (0.907646591371, -0.337048393268, 0.133442885327, -0.045246480208, 0.011169294114, -0.001456501759)
viscosity = 0.05
mean_flow = 0.5
les_time_step = 0.1
ape_time_step = 0.4


def shifted(extended, margin, direction, offset_j):
    width_x = extended.shape[1] - 2 * margin
    width_y = extended.shape[2] - 2 * margin
    if direction == 1:
        return extended[:, margin + offset_j:margin + offset_j + width_x, margin:margin + width_y]
    if direction == 2:
        return extended[:, margin:margin + width_x, margin + offset_j:margin + offset_j + width_y]
    centre = extended[:, margin:margin + width_x, margin:margin + width_y]
    return jnp.roll(centre, -offset_j, axis=3)


def derivative(extended, margin, weight_list, direction):
    total = None
    for offset_j, weight_j in enumerate(weight_list, start=1):
        term = weight_j * (shifted(extended, margin, direction, offset_j) - shifted(extended, margin, direction, -offset_j))
        total = term if total is None else total + term
    return total


def les_tendency(extended, margin):
    grad_x, grad_y, grad_z = [derivative(extended, margin, (0.5,), direction) for direction in (1, 2, 3)]
    centre = shifted(extended, margin, 1, 0)
    vel_x, vel_y, vel_z = centre[0], centre[1], centre[2]
    vort_x = grad_y[2] - grad_z[1]
    vort_y = grad_z[0] - grad_x[2]
    vort_z = grad_x[1] - grad_y[0]
    lamb_vec = jnp.stack([vort_y * vel_z - vort_z * vel_y, vort_z * vel_x - vort_x * vel_z, vort_x * vel_y - vort_y * vel_x])
    spread = -6.0 * centre
    for direction in (1, 2, 3):
        spread = spread + shifted(extended, margin, direction, 1) + shifted(extended, margin, direction, -1)
    tend_vel = -lamb_vec + viscosity * spread[:3]
    tend_scalar = -(vel_x * grad_x[3] + vel_y * grad_y[3] + vel_z * grad_z[3]) + viscosity * spread[3]
    return jnp.concatenate([tend_vel, tend_scalar[None]], axis=0), lamb_vec


def ape_tendency(extended, margin, source):
    grad_x, grad_y, grad_z = [derivative(extended, margin, drp_weights, direction) for direction in (1, 2, 3)]
    tend_press = -mean_flow * grad_x[0] - (grad_x[1] + grad_y[2] + grad_z[3])
    tend_vel = -mean_flow * grad_x[1:] - jnp.stack([grad_x[0], grad_y[0], grad_z[0]]) - source
    return jnp.concatenate([tend_press[None], tend_vel], axis=0)


def extend(whole, margin):
    padded = jnp.pad(whole, ((0, 0), (margin, margin), (0, 0), (0, 0)), mode="wrap")
    return jnp.pad(padded, ((0, 0), (0, 0), (margin, margin), (0, 0)))


def deposit(lamb_vec, block_offset, block_weight):
    block_count = block_offset.shape[0]
    blocks = lamb_vec.reshape(3, block_count, -1)
    anchor = jnp.arange(block_count, dtype=jnp.int32)
    target = (anchor + block_offset) % block_count
    following = (target + 1) % block_count
    columns = jnp.arange(block_count, dtype=jnp.int32)
    matrix = jnp.where(columns[None, :] == target[:, None], block_weight[:, None], 0.0)
    matrix = matrix + jnp.where(columns[None, :] == following[:, None], 1.0 - block_weight[:, None], 0.0)
    moved = jnp.einsum("bs,cbk->csk", matrix, blocks, precision=lax.Precision.HIGHEST)
    return moved.reshape(lamb_vec.shape)


def tendencies(fields, block_offset, block_weight):
    les_part, lamb_vec = les_tendency(extend(fields[0], 1), 1)
    source = deposit(lamb_vec, block_offset, block_weight)
    ape_part = ape_tendency(extend(fields[1], 6), 6, source)
    return jnp.stack([les_part, ape_part])


def reference(flow_state, block_offset, block_weight):
    steps_both = jnp.array([les_time_step, ape_time_step], dtype=flow_state.dtype)[:, None, None, None, None]
    predicted = flow_state + steps_both * tendencies(flow_state, block_offset, block_weight)
    corrected = predicted + steps_both * tendencies(predicted, block_offset, block_weight)
    return 0.5 * (flow_state + corrected)
```

```python
import functools

import jax
import jax.numpy as jnp
from jax import lax
from jax.experimental import pallas as pl
from jax.experimental.pallas import tpu as pltpu
from jax.sharding import PartitionSpec as P

drp_weights = (
    0.907646591371,
    -0.337048393268,
    0.133442885327,
    -0.045246480208,
    0.011169294114,
    -0.001456501759,
)
viscosity = 0.05
mean_flow = 0.5
les_time_step = 0.1
ape_time_step = 0.4

MESH = pl.DeviceIdType.MESH
f32 = jnp.float32

BX = 16
BY = 8
NB = 4
BC = BX // NB
NZ = 128
H = 6

(
    LES_XL, LES_XR, LES_YL, LES_YH,
    PRED_XL, PRED_XR, PRED_YL, PRED_YH,
    RAW_HI, RAW_LO, RAW_NEXT,
    RELAY_HI, RELAY_LO,
    TAB_L, TAB_R,
    A1_XL, A1_XR, A1_YLP, A1_YLV, A1_YHP, A1_YHV,
    A2_XL, A2_XR, A2_YLP, A2_YLV, A2_YHP, A2_YHV,
    EDGE_OWN_L, EDGE_OWN_H, EDGE_NEXT_L, EDGE_NEXT_H, EDGE_PREV_L, EDGE_PREV_H,
    EDGE_P_L, EDGE_P_H,
    N_REMOTE,
) = range(36)
L_FLOW, L_YP, L_YV, L_OFF, L_WT, L_OUT, N_LOCAL = range(7)


def sublane():
    return lax.broadcasted_iota(jnp.int32, (BY, NZ), 0)


def cells_of(first, count):
    return pl.ds(first * BY, count * BY)


def row(ref, f, p):
    return jnp.broadcast_to(ref[f, pl.ds(p, 1), :], (BY, NZ))


def around(cells, low, high, f, plane, edge):
    base = pl.multiple_of(plane * BY, BY)
    centre = cells[f, pl.ds(base, BY), :]
    x_m = cells[f, pl.ds(base - BY, BY), :]
    x_p = cells[f, pl.ds(base + BY, BY), :]
    sub = sublane()
    y_m = jnp.where(sub == 0, row(low, f, edge), pltpu.roll(centre, 1, 0))
    y_p = jnp.where(sub == BY - 1, row(high, f, edge), pltpu.roll(centre, BY - 1, 0))
    z_m = pltpu.roll(centre, 1, 1)
    z_p = pltpu.roll(centre, NZ - 1, 1)
    return centre, x_m, x_p, y_m, y_p, z_m, z_p


def lamb_of(near):
    grad = [
        [0.5 * (n[2] - n[1]), 0.5 * (n[4] - n[3]), 0.5 * (n[6] - n[5])] for n in near[:3]
    ]
    u, v, w = near[0][0], near[1][0], near[2][0]
    vort_x = grad[2][1] - grad[1][2]
    vort_y = grad[0][2] - grad[2][0]
    vort_z = grad[1][0] - grad[0][1]
    lamb = (vort_y * w - vort_z * v, vort_z * u - vort_x * w, vort_x * v - vort_y * u)
    return lamb


def spread_of(n):
    return -6.0 * n[0] + n[2] + n[1] + n[4] + n[3] + n[6] + n[5]


def les_tendency(near):
    lamb = lamb_of(near)
    tend = [-lamb[f] + viscosity * spread_of(near[f]) for f in range(3)]
    if len(near) == 4:
        n = near[3]
        carried = (
            near[0][0] * (0.5 * (n[2] - n[1]))
            + near[1][0] * (0.5 * (n[4] - n[3]))
            + near[2][0] * (0.5 * (n[6] - n[5]))
        )
        tend.append(-carried + viscosity * spread_of(n))
    return tend, lamb


def planes(first, last, unroll, body):
    count = last - first
    assert count % unroll == 0

    def step(i, carry):
        for k in range(unroll):
            body(first + i * unroll + k)
        return carry

    lax.fori_loop(0, count // unroll, step, 0)


def kernel(
    gx_size, gy_size,
    flow, flow_planes, offset, weight, out,
    X, XL, XH, EL, EH, XP, PL, PH, QL, QH,
    F, YE, R, RL, RH, SL, SH, V, VL, VH, WL, WH, LB, G, FP, YP, D, TAB, COEF, O,
    off_s, wt_s, send_sem, recv_sem, local_sem,
):
    grp, gx, gy = lax.axis_index("grp"), lax.axis_index("gx"), lax.axis_index("gy")
    right = lax.rem(gx + 1, gx_size)
    left = lax.rem(gx + gx_size - 1, gx_size)
    has_low, has_high = gy > 0, gy < gy_size - 1
    is_les, is_ape = grp == 0, grp == 1

    def copy(kind, src, dst, device):
        return pltpu.make_async_remote_copy(
            src_ref=src,
            dst_ref=dst,
            send_sem=send_sem.at[kind],
            recv_sem=recv_sem.at[kind],
            device_id=device,
            device_id_type=MESH,
        )

    def here(kind, src, dst):
        return pltpu.make_async_copy(src, dst, local_sem.at[kind])

    me_left, me_right = (grp, left, gy), (grp, right, gy)
    me_low, me_high = (grp, gx, gy - 1), (grp, gx, gy + 1)

    les_first = [
        copy(LES_XL, flow.at[:, cells_of(0, 1)], X.at[:, cells_of(BX + 1, 1)], me_left),
        copy(LES_XR, flow.at[:, cells_of(BX - 1, 1)], X.at[:, cells_of(0, 1)], me_right),
    ]
    les_raw = [
        copy(RAW_HI, flow.at[pl.ds(0, 3), cells_of(8, 8)], R.at[:, cells_of(BX + 8, 8)], (1, gx, gy)),
        copy(RAW_LO, flow.at[pl.ds(0, 3), cells_of(0, 8)], R.at[:, cells_of(BX, 8)], (1, gx, gy)),
        copy(
            RAW_NEXT, flow.at[pl.ds(0, 3), cells_of(0, 14)], R.at[:, cells_of(2 * BX, 14)], (1, left, gy)
        ),
    ]
    les_edge_low = copy(LES_YL, EL, XH, me_low)
    les_edge_high = copy(LES_YH, EH, XL, me_high)
    pred_x = [
        copy(PRED_XL, XP.at[:, cells_of(1, 1)], XP.at[:, cells_of(BX + 1, 1)], me_left),
        copy(PRED_XR, XP.at[:, cells_of(BX, 1)], XP.at[:, cells_of(0, 1)], me_right),
    ]
    pred_low = copy(PRED_YL, QL, PH, me_low)
    pred_high = copy(PRED_YH, QH, PL, me_high)

    relay_hi = copy(RELAY_HI, R.at[:, cells_of(BX + 8, 8)], R.at[:, cells_of(8, 8)], me_right)
    relay_lo = copy(RELAY_LO, R.at[:, cells_of(BX + 2, 6)], R.at[:, cells_of(2, 6)], me_right)
    tables = [
        copy(TAB_L, TAB.at[1], TAB.at[2], me_left),
        copy(TAB_R, TAB.at[1], TAB.at[0], me_right),
    ]
    a1_left = copy(A1_XL, flow.at[:, cells_of(0, H)], F.at[:, cells_of(BX + H, H)], me_left)
    a1_right = copy(A1_XR, flow.at[:, cells_of(BX - H, H)], F.at[:, cells_of(0, H)], me_right)
    low_part, own_part, high_part = pl.ds(0, BY), pl.ds(BY, BY), pl.ds(2 * BY, BY)
    a1_low = [
        copy(A1_YLP, flow_planes.at[0], YE.at[0, :, high_part], me_low),
        copy(A1_YLV, flow_planes.at[2], YE.at[1, :, high_part], me_low),
    ]
    a1_high = [
        copy(A1_YHP, flow_planes.at[0], YE.at[0, :, low_part], me_high),
        copy(A1_YHV, flow_planes.at[2], YE.at[1, :, low_part], me_high),
    ]
    own = cells_of(H, BX)
    a2_left = copy(A2_XL, FP.at[:, cells_of(H, H)], FP.at[:, cells_of(BX + H, H)], me_left)
    a2_right = copy(A2_XR, FP.at[:, cells_of(BX, H)], FP.at[:, cells_of(0, H)], me_right)
    a2_low = [
        copy(A2_YLP, YP.at[0, :, own_part], YP.at[0, :, high_part], me_low),
        copy(A2_YLV, YP.at[1, :, own_part], YP.at[1, :, high_part], me_low),
    ]
    a2_high = [
        copy(A2_YHP, YP.at[0, :, own_part], YP.at[0, :, low_part], me_high),
        copy(A2_YHV, YP.at[1, :, own_part], YP.at[1, :, low_part], me_high),
    ]
    third = [pl.ds(0, BX), pl.ds(BX, BX), pl.ds(2 * BX, BX)]

    def edges(kind_low, kind_high, part):
        return (
            copy(kind_low, SL.at[:, third[part]], RH.at[:, third[part]], me_low),
            copy(kind_high, SH.at[:, third[part]], RL.at[:, third[part]], me_high),
        )

    edge_own = edges(EDGE_OWN_L, EDGE_OWN_H, 1)
    edge_next = edges(EDGE_NEXT_L, EDGE_NEXT_H, 2)
    edge_prev = edges(EDGE_PREV_L, EDGE_PREV_H, 0)
    edge_pred = (copy(EDGE_P_L, WL, VH, me_low), copy(EDGE_P_H, WH, VL, me_high))

    @pl.when(is_les)
    def _():
        here(L_FLOW, flow, X.at[:, cells_of(1, BX)]).start()

    @pl.when(is_ape)
    def _():
        here(L_FLOW, flow, F.at[:, own]).start()
        here(L_YP, flow_planes.at[0], YE.at[0, :, own_part]).start()
        here(L_YV, flow_planes.at[2], YE.at[1, :, own_part]).start()
        here(L_OFF, offset, off_s).start()
        here(L_WT, weight, wt_s).start()

    barrier = pltpu.get_barrier_semaphore()

    def greet(device):
        pl.semaphore_signal(barrier, inc=1, device_id=device, device_id_type=MESH)

    greet(me_left)
    greet(me_right)
    greet((1 - grp, gx, gy))

    @pl.when(is_les)
    def _():
        greet((1, left, gy))

    @pl.when(is_ape)
    def _():
        greet((0, right, gy))

    @pl.when(has_low)
    def _():
        greet(me_low)

    @pl.when(has_high)
    def _():
        greet(me_high)

    zeros_edge = jnp.zeros((48, NZ), f32)

    @pl.when(jnp.logical_not(has_low))
    def _():
        for f in range(4):
            XL[f] = zeros_edge[:BX]
            PL[f] = zeros_edge[:BX]
        for f in range(3):
            RL[f] = zeros_edge
            VL[f] = zeros_edge
        for f in range(2):
            YE[f, :, pl.ds(0, BY)] = jnp.zeros((BX, BY, NZ), f32)
            YP[f, :, pl.ds(0, BY)] = jnp.zeros((BX, BY, NZ), f32)

    @pl.when(jnp.logical_not(has_high))
    def _():
        for f in range(4):
            XH[f] = zeros_edge[:BX]
            PH[f] = zeros_edge[:BX]
        for f in range(3):
            RH[f] = zeros_edge
            VH[f] = zeros_edge
        for f in range(2):
            YE[f, :, pl.ds(2 * BY, BY)] = jnp.zeros((BX, BY, NZ), f32)
            YP[f, :, pl.ds(2 * BY, BY)] = jnp.zeros((BX, BY, NZ), f32)

    y_neighbours = jnp.where(has_low, 1, 0) + jnp.where(has_high, 1, 0)

    def exchange(low, high, what):
        @pl.when(has_low)
        def _():
            getattr(low, what)()

        @pl.when(has_high)
        def _():
            getattr(high, what)()

    def pack(cells, first, count, low, high, at, fields):
        for f in range(fields):
            low[f, pl.ds(at, count), :] = cells[f, pl.ds(first * BY, count, stride=BY), :]
            high[f, pl.ds(at, count), :] = cells[
                f, pl.ds(first * BY + BY - 1, count, stride=BY), :
            ]

    @pl.when(is_les)
    def les():
        pl.semaphore_wait(barrier, 4 + y_neighbours)
        for c in les_first + les_raw:
            c.start()
        cells, ahead, final = X, XP, O
        here(L_FLOW, flow, X.at[:, cells_of(1, BX)]).wait()
        pack(cells, 1, BX, EL, EH, 0, 4)
        exchange(les_edge_low, les_edge_high, "start")
        for c in les_first:
            c.wait_recv()
        exchange(les_edge_high, les_edge_low, "wait_recv")

        def predict(x):
            near = [around(cells, XL, XH, f, x + 1, x) for f in range(4)]
            tend, _ = les_tendency(near)
            for f in range(4):
                ahead[f, pl.ds(pl.multiple_of((x + 1) * BY, BY), BY), :] = (
                    near[f][0] + les_time_step * tend[f]
                )

        planes(0, BX, 2, predict)
        for c in pred_x:
            c.start()
        pack(ahead, 1, BX, QL, QH, 0, 4)
        exchange(pred_low, pred_high, "start")
        for c in pred_x:
            c.wait_recv()
        exchange(pred_high, pred_low, "wait_recv")

        def correct(x):
            near = [around(ahead, PL, PH, f, x + 1, x) for f in range(4)]
            tend, _ = les_tendency(near)
            for f in range(4):
                before = cells[f, pl.ds(pl.multiple_of((x + 1) * BY, BY), BY), :]
                final[f, pl.ds(pl.multiple_of(x * BY, BY), BY), :] = 0.5 * (
                    before + near[f][0] + les_time_step * tend[f]
                )

        planes(0, BX, 2, correct)
        here(L_OUT, O, out).start()
        for c in les_first + les_raw + pred_x:
            c.wait_send()
        exchange(les_edge_low, les_edge_high, "wait_send")
        exchange(pred_low, pred_high, "wait_send")
        here(L_OUT, O, out).wait()

    @pl.when(is_ape)
    def ape():
        raw, state, ahead, moved, rate, state_p, dep, final = R, F, V, LB, G, FP, D, O

        here(L_OFF, offset, off_s).wait()
        here(L_WT, weight, wt_s).wait()
        sub = sublane()
        table = jnp.zeros((BY, NZ), f32)
        for b in range(NB):
            table = jnp.where(sub == b, off_s[b].astype(f32), table)
            table = jnp.where(sub == NB + b, wt_s[b], table)
        TAB[1] = table

        pl.semaphore_wait(barrier, 4 + y_neighbours)
        a1_left.start()
        for low, high in zip(a1_low, a1_high):
            exchange(low, high, "start")
        for c in tables:
            c.start()

        les_raw[0].wait_recv()
        relay_hi.start()
        les_raw[1].wait_recv()
        relay_lo.start()
        a1_right.start()
        pack(raw, BX, BX, SL, SH, BX, 3)
        exchange(*edge_own, "start")

        here(L_FLOW, flow, F.at[:, own]).wait()
        here(L_YP, flow_planes.at[0], YE.at[0, :, own_part]).wait()
        here(L_YV, flow_planes.at[2], YE.at[1, :, own_part]).wait()

        def thirteen(plus, minus):
            total = None
            for j, c in enumerate(drp_weights, start=1):
                term = c * (plus(j) - minus(j))
                total = term if total is None else total + term
            return total

        def rate_yz(cells, walls):
            def body(x):
                at = pl.multiple_of((x + H) * BY, BY)
                to = pl.ds(pl.multiple_of(x * BY, BY), BY)
                p, w = cells[0, pl.ds(at, BY), :], cells[3, pl.ds(at, BY), :]
                dz = [
                    thirteen(lambda j: pltpu.roll(q, NZ - j, 1), lambda j: pltpu.roll(q, j, 1))
                    for q in (p, w)
                ]
                dy = [
                    thirteen(
                        lambda j: walls[f, x, pl.ds(BY + j, BY), :],
                        lambda j: walls[f, x, pl.ds(BY - j, BY), :],
                    )
                    for f in range(2)
                ]
                rate[0, to, :] = -(dy[1] + dz[1])
                rate[2, to, :] = -dy[0]
                rate[3, to, :] = -dz[0]

            planes(0, BX, 2, body)

        def rate_x(cells, x):
            at = (x + H) * BY

            def along(f):
                return thirteen(
                    lambda j: cells[f, pl.ds(pl.multiple_of(at + j * BY, BY), BY), :],
                    lambda j: cells[f, pl.ds(pl.multiple_of(at - j * BY, BY), BY), :],
                )

            to = pl.ds(pl.multiple_of(x * BY, BY), BY)
            dx = [along(f) for f in range(4)]
            return (
                rate[0, to, :] - mean_flow * dx[0] - dx[1],
                -mean_flow * dx[1] - dx[0],
                rate[2, to, :] - mean_flow * dx[2],
                rate[3, to, :] - mean_flow * dx[3],
            )

        for low, high in zip(a1_low, a1_high):
            exchange(high, low, "wait_recv")
        rate_yz(state, YE)

        les_raw[2].wait_recv()
        pack(raw, 2 * BX, BX, SL, SH, 2 * BX, 3)
        exchange(*edge_next, "start")

        for c in tables:
            c.wait_recv()
        pairs = []
        for d in range(NB):
            for part, shift in enumerate((NB, 0, -NB)):
                for b in range(NB):
                    near_block, far_block = 1 - NB, NB
                    lowest = b + (near_block if b < NB - 1 else 0)
                    highest = b + (far_block if b > 0 else 0)
                    if lowest <= d + shift <= highest:
                        pairs.append((d, part, b, d + shift))
        for k, (d, part, b, aim) in enumerate(pairs):
            target = row(TAB, part, b) + float(b)
            share = row(TAB, part, NB + b)
            COEF[k] = jnp.where(target == float(aim), share, 0.0) + jnp.where(
                target + 1.0 == float(aim), 1.0 - share, 0.0
            )

        def first_lamb(p):
            near = [around(raw, RL, RH, f, p, p) for f in range(3)]
            tend, lamb = les_tendency(near)
            to = pl.ds(pl.multiple_of(p * BY, BY), BY)
            for f in range(3):
                ahead[f, to, :] = near[f][0] + les_time_step * tend[f]
                moved[f, to, :] = lamb[f]

        def second_lamb(p):
            near = [around(ahead, VL, VH, f, p, p) for f in range(3)]
            lamb = lamb_of(near)
            to = pl.ds(pl.multiple_of(p * BY, BY), BY)
            for f in range(3):
                moved[f, to, :] = lamb[f]

        def deposit():
            for d in range(NB):
                terms = [(k, q[1] * BX + q[2] * BC) for k, q in enumerate(pairs) if q[0] == d]

                def body(r, carry):
                    for f in range(3):
                        total = None
                        for k, first in terms:
                            at = pl.multiple_of((first + r) * BY, BY)
                            term = COEF[k] * moved[f, pl.ds(at, BY), :]
                            total = term if total is None else total + term
                        to = pl.multiple_of((d * BC + r) * BY, BY)
                        dep[f, pl.ds(to, BY), :] = total
                    return carry

                lax.fori_loop(0, BC, body, 0)

        exchange(edge_own[1], edge_own[0], "wait_recv")
        exchange(edge_next[1], edge_next[0], "wait_recv")
        planes(BX + 1, BX + 29, 2, first_lamb)

        relay_hi.wait_recv()
        relay_lo.wait_recv()
        pack(raw, 0, BX, SL, SH, 0, 3)
        exchange(*edge_prev, "start")
        exchange(edge_prev[1], edge_prev[0], "wait_recv")
        planes(3, BX + 1, 2, first_lamb)
        pack(ahead, 0, 3 * BX, WL, WH, 0, 3)
        exchange(*edge_pred, "start")
        deposit()

        a1_left.wait_recv()
        a1_right.wait_recv()

        def predict(x):
            tend = rate_x(state, x)
            at = pl.ds(pl.multiple_of((x + H) * BY, BY), BY)
            to = pl.ds(pl.multiple_of(x * BY, BY), BY)
            for f in range(4):
                t = tend[f] - dep[f - 1, to, :] if f else tend[f]
                predicted = state[f, at, :] + ape_time_step * t
                state_p[f, at, :] = predicted
                if f in (0, 2):
                    YP[f // 2, x, own_part, :] = predicted

        planes(0, BX, 2, predict)
        a2_left.start()
        a2_right.start()
        for low, high in zip(a2_low, a2_high):
            exchange(low, high, "start")

        exchange(edge_pred[1], edge_pred[0], "wait_recv")
        planes(4, 44, 2, second_lamb)
        deposit()
        for low, high in zip(a2_low, a2_high):
            exchange(high, low, "wait_recv")
        rate_yz(state_p, YP)
        a2_left.wait_recv()
        a2_right.wait_recv()

        def correct(x):
            tend = rate_x(state_p, x)
            at = pl.ds(pl.multiple_of((x + H) * BY, BY), BY)
            to = pl.ds(pl.multiple_of(x * BY, BY), BY)
            for f in range(4):
                t = tend[f] - dep[f - 1, to, :] if f else tend[f]
                final[f, to, :] = 0.5 * (
                    state[f, at, :] + state_p[f, at, :] + ape_time_step * t
                )

        planes(0, BX, 2, correct)
        here(L_OUT, O, out).start()
        for c in tables + [relay_hi, relay_lo, a1_left, a1_right, a2_left, a2_right]:
            c.wait_send()
        for pair in (edge_own, edge_next, edge_prev, edge_pred):
            exchange(*pair, "wait_send")
        for lows, highs in ((a1_low, a1_high), (a2_low, a2_high)):
            for low, high in zip(lows, highs):
                exchange(low, high, "wait_send")
        here(L_OUT, O, out).wait()


def on_device(flow_state, block_offset, block_weight):
    gx_size, gy_size = lax.axis_size("gx"), lax.axis_size("gy")

    def vmem(*shape):
        return pltpu.VMEM(shape, f32)

    def planes_of(fields, count):
        return vmem(fields, count * BY, NZ)

    scratch = [
        planes_of(4, BX + 2),
        *[vmem(4, BX, NZ)] * 4,
        planes_of(4, BX + 2),
        *[vmem(4, BX, NZ)] * 4,
        planes_of(4, BX + 2 * H),
        vmem(2, BX, 3 * BY, NZ),
        planes_of(3, 3 * BX),
        *[vmem(3, 3 * BX, NZ)] * 4,
        planes_of(3, 3 * BX),
        *[vmem(3, 3 * BX, NZ)] * 4,
        planes_of(3, 3 * BX),
        planes_of(4, BX),
        planes_of(4, BX + 2 * H),
        vmem(2, BX, 3 * BY, NZ),
        planes_of(3, BX),
        vmem(3, BY, NZ),
        vmem(25, BY, NZ),
        planes_of(4, BX),
        pltpu.SMEM((NB,), jnp.int32),
        pltpu.SMEM((NB,), f32),
        pltpu.SemaphoreType.DMA((N_REMOTE,)),
        pltpu.SemaphoreType.DMA((N_REMOTE,)),
        pltpu.SemaphoreType.DMA((N_LOCAL,)),
    ]
    anywhere = pl.BlockSpec(memory_space=pl.ANY)
    advanced = pl.pallas_call(
        functools.partial(kernel, gx_size, gy_size),
        out_shape=jax.ShapeDtypeStruct((4, BX * BY, NZ), f32),
        in_specs=[anywhere] * 4,
        out_specs=anywhere,
        scratch_shapes=scratch,
        compiler_params=pltpu.CompilerParams(collective_id=0, has_side_effects=True),
        name="heun",
    )(flow_state.reshape(4, BX * BY, NZ), flow_state[0], block_offset, block_weight)
    return advanced.reshape(flow_state.shape)


def solution(mesh):
    placed = (P("grp", None, "gx", "gy", None), P("gx"), P("gx"))
    return jax.shard_map(
        on_device,
        mesh=mesh,
        in_specs=placed,
        out_specs=P("grp", None, "gx", "gy", None),
        check_vma=False,
    )
```

```python
import functools

import jax
import jax.numpy as jnp
from jax import lax
from jax.experimental import pallas as pl
from jax.experimental.pallas import tpu as pltpu
from jax.sharding import PartitionSpec as P

drp_weights = (
    0.907646591371,
    -0.337048393268,
    0.133442885327,
    -0.045246480208,
    0.011169294114,
    -0.001456501759,
)
viscosity = 0.05
mean_flow = 0.5
les_time_step = 0.1
ape_time_step = 0.4

MESH = pl.DeviceIdType.MESH
f32 = jnp.float32

BX = 16
BY = 8
NB = 4
BC = BX // NB
NZ = 128
H = 6

(
    LES_XL, LES_XR, LES_YL, LES_YH,
    PRED_XL, PRED_XR, PRED_YL, PRED_YH,
    RAW_0, RAW_1, RAW_2, RAW_3, RAW_NEXT,
    RELAY_0, RELAY_1, RELAY_2, RELAY_3,
    TAB_L, TAB_R,
    A1_XL, A1_XR, A1_YLP, A1_YLV, A1_YHP, A1_YHV,
    A2_XL, A2_XR, A2_XLP, A2_XRP, A2_YLP, A2_YLV, A2_YHP, A2_YHV,
    EDGE_OWN_L, EDGE_OWN_H, EDGE_NEXT_L, EDGE_NEXT_H, EDGE_PREV_L, EDGE_PREV_H,
    EDGE_P_L, EDGE_P_H, LATE_P_L, LATE_P_H,
    N_REMOTE,
) = range(44)
L_FLOW, L_YP, L_YV, L_OFF, L_WT, L_OUT, N_LOCAL = range(7)


def sublane():
    return lax.broadcasted_iota(jnp.int32, (BY, NZ), 0)


def cells_of(first, count):
    return pl.ds(first * BY, count * BY)


def row(ref, f, p):
    return jnp.broadcast_to(ref[f, pl.ds(p, 1), :], (BY, NZ))


def around(cells, low, high, f, plane, edge):
    base = pl.multiple_of(plane * BY, BY)
    centre = cells[f, pl.ds(base, BY), :]
    x_m = cells[f, pl.ds(base - BY, BY), :]
    x_p = cells[f, pl.ds(base + BY, BY), :]
    sub = sublane()
    y_m = jnp.where(sub == 0, row(low, f, edge), pltpu.roll(centre, 1, 0))
    y_p = jnp.where(sub == BY - 1, row(high, f, edge), pltpu.roll(centre, BY - 1, 0))
    z_m = pltpu.roll(centre, 1, 1)
    z_p = pltpu.roll(centre, NZ - 1, 1)
    return centre, x_m, x_p, y_m, y_p, z_m, z_p


def lamb_of(near):
    grad = [
        [0.5 * (n[2] - n[1]), 0.5 * (n[4] - n[3]), 0.5 * (n[6] - n[5])] for n in near[:3]
    ]
    u, v, w = near[0][0], near[1][0], near[2][0]
    vort_x = grad[2][1] - grad[1][2]
    vort_y = grad[0][2] - grad[2][0]
    vort_z = grad[1][0] - grad[0][1]
    lamb = (vort_y * w - vort_z * v, vort_z * u - vort_x * w, vort_x * v - vort_y * u)
    return lamb


def spread_of(n):
    return -6.0 * n[0] + n[2] + n[1] + n[4] + n[3] + n[6] + n[5]


def les_tendency(near):
    lamb = lamb_of(near)
    tend = [-lamb[f] + viscosity * spread_of(near[f]) for f in range(3)]
    if len(near) == 4:
        n = near[3]
        carried = (
            near[0][0] * (0.5 * (n[2] - n[1]))
            + near[1][0] * (0.5 * (n[4] - n[3]))
            + near[2][0] * (0.5 * (n[6] - n[5]))
        )
        tend.append(-carried + viscosity * spread_of(n))
    return tend, lamb


def planes(first, last, unroll, body):
    count = last - first
    assert count % unroll == 0

    def step(i, carry):
        for k in range(unroll):
            body(first + i * unroll + k)
        return carry

    lax.fori_loop(0, count // unroll, step, 0)


def kernel(
    gx_size, gy_size,
    flow, flow_planes, offset, weight, out,
    X, XL, XH, EL, EH, XP, PL, PH, QL, QH,
    F, YE, R, RL, RH, V, VL, VH, WL, WH, LB, LC, G, FP, YP, D, E, TAB, COEF,
    off_s, wt_s, send_sem, recv_sem, local_sem,
):
    grp, gx, gy = lax.axis_index("grp"), lax.axis_index("gx"), lax.axis_index("gy")
    right = lax.rem(gx + 1, gx_size)
    left = lax.rem(gx + gx_size - 1, gx_size)
    has_low, has_high = gy > 0, gy < gy_size - 1
    is_les, is_ape = grp == 0, grp == 1

    def copy(kind, src, dst, device):
        return pltpu.make_async_remote_copy(
            src_ref=src,
            dst_ref=dst,
            send_sem=send_sem.at[kind],
            recv_sem=recv_sem.at[kind],
            device_id=device,
            device_id_type=MESH,
        )

    def here(kind, src, dst):
        return pltpu.make_async_copy(src, dst, local_sem.at[kind])

    me_left, me_right = (grp, left, gy), (grp, right, gy)
    me_low, me_high = (grp, gx, gy - 1), (grp, gx, gy + 1)

    les_first = [
        copy(LES_XL, flow.at[:, cells_of(0, 1)], X.at[:, cells_of(BX + 1, 1)], me_left),
        copy(LES_XR, flow.at[:, cells_of(BX - 1, 1)], X.at[:, cells_of(0, 1)], me_right),
    ]
    pieces = [(12, 4), (8, 4), (4, 4), (0, 4)]
    velocity = pl.ds(0, 3)
    les_raw = [
        copy(
            RAW_0 + k,
            flow.at[velocity, cells_of(first, count)],
            R.at[:, cells_of(BX + first, count)],
            (1, gx, gy),
        )
        for k, (first, count) in enumerate(pieces)
    ]
    les_next = copy(
        RAW_NEXT, flow.at[velocity, cells_of(0, 14)], R.at[:, cells_of(2 * BX, 14)], (1, left, gy)
    )
    les_edge_low = copy(LES_YL, EL, XH, me_low)
    les_edge_high = copy(LES_YH, EH, XL, me_high)
    pred_x = [
        copy(PRED_XL, XP.at[:, cells_of(1, 1)], XP.at[:, cells_of(BX + 1, 1)], me_left),
        copy(PRED_XR, XP.at[:, cells_of(BX, 1)], XP.at[:, cells_of(0, 1)], me_right),
    ]
    pred_low = copy(PRED_YL, QL, PH, me_low)
    pred_high = copy(PRED_YH, QH, PL, me_high)

    relays = []
    for k, (first, count) in enumerate(pieces):
        start = max(first, 2)
        count = first + count - start
        relays.append(
            copy(
                RELAY_0 + k,
                R.at[:, cells_of(BX + start, count)],
                R.at[:, cells_of(start, count)],
                me_right,
            )
        )
    tables = [
        copy(TAB_L, TAB.at[1], TAB.at[2], me_left),
        copy(TAB_R, TAB.at[1], TAB.at[0], me_right),
    ]
    a1_left = copy(A1_XL, flow.at[:, cells_of(0, H)], F.at[:, cells_of(BX + H, H)], me_left)
    a1_right = copy(A1_XR, flow.at[:, cells_of(BX - H, H)], F.at[:, cells_of(0, H)], me_right)
    low_part, own_part, high_part = pl.ds(0, BY), pl.ds(BY, BY), pl.ds(2 * BY, BY)
    a1_low = [
        copy(A1_YLP, flow_planes.at[0], YE.at[0, :, high_part], me_low),
        copy(A1_YLV, flow_planes.at[2], YE.at[1, :, high_part], me_low),
    ]
    a1_high = [
        copy(A1_YHP, flow_planes.at[0], YE.at[0, :, low_part], me_high),
        copy(A1_YHV, flow_planes.at[2], YE.at[1, :, low_part], me_high),
    ]
    own = cells_of(H, BX)
    flows = pl.ds(1, 3)
    a2_left = copy(A2_XL, FP.at[flows, cells_of(H, H)], FP.at[flows, cells_of(BX + H, H)], me_left)
    a2_right = copy(A2_XR, FP.at[flows, cells_of(BX, H)], FP.at[flows, cells_of(0, H)], me_right)
    a2_left_p = copy(A2_XLP, FP.at[0, cells_of(H, H)], FP.at[0, cells_of(BX + H, H)], me_left)
    a2_right_p = copy(A2_XRP, FP.at[0, cells_of(BX, H)], FP.at[0, cells_of(0, H)], me_right)
    a2_low = [
        copy(A2_YLP, YP.at[0, :, own_part], YP.at[0, :, high_part], me_low),
        copy(A2_YLV, YP.at[1, :, own_part], YP.at[1, :, high_part], me_low),
    ]
    a2_high = [
        copy(A2_YHP, YP.at[0, :, own_part], YP.at[0, :, low_part], me_high),
        copy(A2_YHV, YP.at[1, :, own_part], YP.at[1, :, low_part], me_high),
    ]
    third = [pl.ds(0, BX), pl.ds(BX, BX), pl.ds(2 * BX, BX)]

    edge_own = (
        copy(EDGE_OWN_L, EL.at[velocity], RH.at[:, third[1]], (1, gx, gy - 1)),
        copy(EDGE_OWN_H, EH.at[velocity], RL.at[:, third[1]], (1, gx, gy + 1)),
    )
    edge_next = (
        copy(EDGE_NEXT_L, EL.at[velocity], RH.at[:, third[2]], (1, left, gy - 1)),
        copy(EDGE_NEXT_H, EH.at[velocity], RL.at[:, third[2]], (1, left, gy + 1)),
    )
    edge_prev = (
        copy(EDGE_PREV_L, RL.at[:, third[1]], RL.at[:, third[0]], me_right),
        copy(EDGE_PREV_H, RH.at[:, third[1]], RH.at[:, third[0]], me_right),
    )
    soon, late = pl.ds(BX, 2 * BX), pl.ds(0, BX)
    edge_pred = (
        copy(EDGE_P_L, WL.at[:, soon], VH.at[:, soon], me_low),
        copy(EDGE_P_H, WH.at[:, soon], VL.at[:, soon], me_high),
    )
    late_pred = (
        copy(LATE_P_L, WL.at[:, late], VH.at[:, late], me_low),
        copy(LATE_P_H, WH.at[:, late], VL.at[:, late], me_high),
    )

    @pl.when(is_les)
    def _():
        here(L_FLOW, flow, X.at[:, cells_of(1, BX)]).start()

    @pl.when(is_ape)
    def _():
        here(L_FLOW, flow, F.at[:, own]).start()
        here(L_YP, flow_planes.at[0], YE.at[0, :, own_part]).start()
        here(L_YV, flow_planes.at[2], YE.at[1, :, own_part]).start()
        here(L_OFF, offset, off_s).start()
        here(L_WT, weight, wt_s).start()

    barrier = pltpu.get_barrier_semaphore()

    def greet(device):
        pl.semaphore_signal(barrier, inc=1, device_id=device, device_id_type=MESH)

    greet(me_left)
    greet(me_right)
    greet((1 - grp, gx, gy))

    @pl.when(is_les)
    def _():
        greet((1, left, gy))

        @pl.when(has_low)
        def _():
            greet((1, gx, gy - 1))
            greet((1, left, gy - 1))

        @pl.when(has_high)
        def _():
            greet((1, gx, gy + 1))
            greet((1, left, gy + 1))

    @pl.when(is_ape)
    def _():
        greet((0, right, gy))

        @pl.when(has_low)
        def _():
            greet((0, gx, gy - 1))
            greet((0, right, gy - 1))

        @pl.when(has_high)
        def _():
            greet((0, gx, gy + 1))
            greet((0, right, gy + 1))

    @pl.when(has_low)
    def _():
        greet(me_low)

    @pl.when(has_high)
    def _():
        greet(me_high)

    zeros_edge = jnp.zeros((48, NZ), f32)

    @pl.when(jnp.logical_not(has_low))
    def _():
        for f in range(4):
            XL[f] = zeros_edge[:BX]
            PL[f] = zeros_edge[:BX]
        for f in range(3):
            RL[f] = zeros_edge
            VL[f] = zeros_edge
        for f in range(2):
            YE[f, :, pl.ds(0, BY)] = jnp.zeros((BX, BY, NZ), f32)
            YP[f, :, pl.ds(0, BY)] = jnp.zeros((BX, BY, NZ), f32)

    @pl.when(jnp.logical_not(has_high))
    def _():
        for f in range(4):
            XH[f] = zeros_edge[:BX]
            PH[f] = zeros_edge[:BX]
        for f in range(3):
            RH[f] = zeros_edge
            VH[f] = zeros_edge
        for f in range(2):
            YE[f, :, pl.ds(2 * BY, BY)] = jnp.zeros((BX, BY, NZ), f32)
            YP[f, :, pl.ds(2 * BY, BY)] = jnp.zeros((BX, BY, NZ), f32)

    y_neighbours = jnp.where(has_low, 1, 0) + jnp.where(has_high, 1, 0)

    def exchange(low, high, what):
        @pl.when(has_low)
        def _():
            getattr(low, what)()

        @pl.when(has_high)
        def _():
            getattr(high, what)()

    def pack(cells, first, count, low, high, at, fields):
        for f in range(fields):
            low[f, pl.ds(at, count), :] = cells[f, pl.ds(first * BY, count, stride=BY), :]
            high[f, pl.ds(at, count), :] = cells[
                f, pl.ds(first * BY + BY - 1, count, stride=BY), :
            ]

    @pl.when(is_les)
    def les():
        cells, ahead, final = X, XP, out
        here(L_FLOW, flow, X.at[:, cells_of(1, BX)]).wait()
        pack(cells, 1, BX, EL, EH, 0, 4)
        pl.semaphore_wait(barrier, 4 + 3 * y_neighbours)
        exchange(*edge_own, "start")
        exchange(*edge_next, "start")
        for c in les_raw + [les_next] + les_first:
            c.start()
        exchange(les_edge_low, les_edge_high, "start")
        for c in les_first:
            c.wait_recv()
        exchange(les_edge_high, les_edge_low, "wait_recv")

        def predict(x):
            near = [around(cells, XL, XH, f, x + 1, x) for f in range(4)]
            tend, _ = les_tendency(near)
            for f in range(4):
                ahead[f, pl.ds(pl.multiple_of((x + 1) * BY, BY), BY), :] = (
                    near[f][0] + les_time_step * tend[f]
                )

        planes(0, BX, 2, predict)
        for c in pred_x:
            c.start()
        pack(ahead, 1, BX, QL, QH, 0, 4)
        exchange(pred_low, pred_high, "start")
        for c in pred_x:
            c.wait_recv()
        exchange(pred_high, pred_low, "wait_recv")

        def correct(x):
            near = [around(ahead, PL, PH, f, x + 1, x) for f in range(4)]
            tend, _ = les_tendency(near)
            for f in range(4):
                before = cells[f, pl.ds(pl.multiple_of((x + 1) * BY, BY), BY), :]
                final[f, pl.ds(pl.multiple_of(x * BY, BY), BY), :] = 0.5 * (
                    before + near[f][0] + les_time_step * tend[f]
                )

        planes(0, BX, 2, correct)
        for c in les_raw + [les_next] + les_first + pred_x:
            c.wait_send()
        exchange(les_edge_low, les_edge_high, "wait_send")
        exchange(pred_low, pred_high, "wait_send")
        exchange(*edge_own, "wait_send")
        exchange(*edge_next, "wait_send")

    @pl.when(is_ape)
    def ape():
        raw, state, ahead, rate, state_p, final = R, F, V, G, FP, out

        here(L_OFF, offset, off_s).wait()
        here(L_WT, weight, wt_s).wait()
        sub = sublane()
        table = jnp.zeros((BY, NZ), f32)
        for b in range(NB):
            table = jnp.where(sub == b, off_s[b].astype(f32), table)
            table = jnp.where(sub == NB + b, wt_s[b], table)
        TAB[1] = table

        pl.semaphore_wait(barrier, 4 + 3 * y_neighbours)
        for c in tables:
            c.start()
        a1_right.start()
        a1_left.start()
        for low, high in zip(a1_low, a1_high):
            exchange(low, high, "start")

        def thirteen(plus, minus):
            total = None
            for j, c in enumerate(drp_weights, start=1):
                term = c * (plus(j) - minus(j))
                total = term if total is None else total + term
            return total

        def rate_z(cells):
            def body(x):
                at = pl.multiple_of((x + H) * BY, BY)
                to = pl.ds(pl.multiple_of(x * BY, BY), BY)
                p, w = cells[0, pl.ds(at, BY), :], cells[3, pl.ds(at, BY), :]
                dz = [
                    thirteen(lambda j: pltpu.roll(q, NZ - j, 1), lambda j: pltpu.roll(q, j, 1))
                    for q in (p, w)
                ]
                rate[0, to, :] = -dz[1]
                rate[3, to, :] = -dz[0]

            planes(0, BX, 2, body)

        def rate_y(walls):
            def body(x):
                to = pl.ds(pl.multiple_of(x * BY, BY), BY)
                dy = [
                    thirteen(
                        lambda j: walls[f, x, pl.ds(BY + j, BY), :],
                        lambda j: walls[f, x, pl.ds(BY - j, BY), :],
                    )
                    for f in range(2)
                ]
                rate[0, to, :] = rate[0, to, :] - dy[1]
                rate[2, to, :] = -dy[0]

            planes(0, BX, 2, body)

        def rate_x(cells, x):
            at = (x + H) * BY

            def along(f):
                return thirteen(
                    lambda j: cells[f, pl.ds(pl.multiple_of(at + j * BY, BY), BY), :],
                    lambda j: cells[f, pl.ds(pl.multiple_of(at - j * BY, BY), BY), :],
                )

            to = pl.ds(pl.multiple_of(x * BY, BY), BY)
            dx = [along(f) for f in range(4)]
            return (
                rate[0, to, :] - mean_flow * dx[0] - dx[1],
                -mean_flow * dx[1] - dx[0],
                rate[2, to, :] - mean_flow * dx[2],
                rate[3, to, :] - mean_flow * dx[3],
            )

        here(L_FLOW, flow, F.at[:, own]).wait()
        rate_z(state)

        pairs = []
        for d in range(NB):
            for part, shift in enumerate((NB, 0, -NB)):
                for b in range(NB):
                    near_block, far_block = 1 - NB, NB
                    lowest = b + (near_block if b < NB - 1 else 0)
                    highest = b + (far_block if b > 0 else 0)
                    if lowest <= d + shift <= highest:
                        pairs.append((d, part, b, d + shift))

        def first_lamb(p):
            near = [around(raw, RL, RH, f, p, p) for f in range(3)]
            tend, lamb = les_tendency(near)
            to = pl.ds(pl.multiple_of(p * BY, BY), BY)
            for f in range(3):
                ahead[f, to, :] = near[f][0] + les_time_step * tend[f]
                LB[f, to, :] = lamb[f]

        def second_lamb(p):
            near = [around(ahead, VL, VH, f, p, p - 1) for f in range(3)]
            lamb = lamb_of(near)
            to = pl.ds(pl.multiple_of(p * BY, BY), BY)
            for f in range(3):
                LC[f, to, :] = lamb[f]

        def deposit(moved, is_late, add):
            for d in range(NB):
                terms = [
                    (k, part * BX + b * BC)
                    for k, (to, part, b, _) in enumerate(pairs)
                    if to == d and is_late == (part * NB + b <= NB)
                ]

                def body(r, carry):
                    for f in range(3):
                        total = None
                        for k, first in terms:
                            at = pl.multiple_of((first + r) * BY, BY)
                            term = COEF[k] * moved[f, pl.ds(at, BY), :]
                            total = term if total is None else total + term
                        add(f, d * BC + r, total)
                    return carry

                lax.fori_loop(0, BC, body, 0)

        def keep_in(ref):
            def add(f, x, total):
                ref[f, pl.ds(pl.multiple_of(x * BY, BY), BY), :] = total

            return add

        exchange(edge_own[1], edge_own[0], "wait_recv")
        exchange(*edge_prev, "start")
        for k in range(2):
            les_raw[k].wait_recv()
            relays[k].start()
        planes(BX + 9, BX + 15, 2, first_lamb)
        les_raw[2].wait_recv()
        relays[2].start()
        planes(BX + 5, BX + 9, 2, first_lamb)
        les_raw[3].wait_recv()
        relays[3].start()
        planes(BX + 1, BX + 5, 2, first_lamb)

        exchange(edge_next[1], edge_next[0], "wait_recv")
        les_next.wait_recv()
        planes(2 * BX - 1, 2 * BX + 13, 2, first_lamb)
        pack(ahead, BX + 1, 28, WL, WH, BX, 3)
        exchange(*edge_pred, "start")
        for c in tables:
            c.wait_recv()
        for k, (d, part, b, aim) in enumerate(pairs):
            target = row(TAB, part, b) + float(b)
            share = row(TAB, part, NB + b)
            COEF[k] = jnp.where(target == float(aim), share, 0.0) + jnp.where(
                target + 1.0 == float(aim), 1.0 - share, 0.0
            )
        deposit(LB, False, keep_in(D))

        here(L_YP, flow_planes.at[0], YE.at[0, :, own_part]).wait()
        here(L_YV, flow_planes.at[2], YE.at[1, :, own_part]).wait()
        for low, high in zip(a1_low, a1_high):
            exchange(high, low, "wait_recv")
        rate_y(YE)

        exchange(*edge_prev, "wait_recv")
        for k, (first, last) in enumerate(((13, 17), (9, 13), (5, 9), (3, 5))):
            relays[k].wait_recv()
            planes(first, last, 2, first_lamb)

        a1_left.wait_recv()
        a1_right.wait_recv()

        def predict(x):
            tend = rate_x(state, x)
            at = pl.ds(pl.multiple_of((x + H) * BY, BY), BY)
            to = pl.ds(pl.multiple_of(x * BY, BY), BY)
            for f in range(4):
                t = tend[f] - D[f - 1, to, :] if f else tend[f]
                predicted = state[f, at, :] + ape_time_step * t
                state_p[f, at, :] = predicted
                if f == 0:
                    YP[0, x, own_part, :] = predicted

        planes(0, BX, 2, predict)
        a2_left_p.start()
        a2_right_p.start()
        exchange(a2_low[0], a2_high[0], "start")

        def take_source(f, x, total):
            at = pl.ds(pl.multiple_of((x + H) * BY, BY), BY)
            predicted = state_p[f + 1, at, :] - ape_time_step * total
            state_p[f + 1, at, :] = predicted
            if f == 1:
                YP[1, x, own_part, :] = predicted

        deposit(LB, True, take_source)
        a2_left.start()
        a2_right.start()
        exchange(a2_low[1], a2_high[1], "start")
        pack(ahead, 1, BX, WL, WH, 0, 3)
        exchange(*late_pred, "start")

        rate_z(state_p)
        exchange(edge_pred[1], edge_pred[0], "wait_recv")
        planes(BX + 2, BX + 28, 2, second_lamb)
        deposit(LC, False, keep_in(E))
        for low, high in zip(a2_low, a2_high):
            exchange(high, low, "wait_recv")
        rate_y(YP)

        def more_source(f, x, total):
            to = pl.ds(pl.multiple_of(x * BY, BY), BY)
            E[f, to, :] = E[f, to, :] + total

        exchange(late_pred[1], late_pred[0], "wait_recv")
        planes(4, BX + 2, 2, second_lamb)
        deposit(LC, True, more_source)
        for c in (a2_left_p, a2_right_p, a2_left, a2_right):
            c.wait_recv()

        def correct(x):
            tend = rate_x(state_p, x)
            at = pl.ds(pl.multiple_of((x + H) * BY, BY), BY)
            to = pl.ds(pl.multiple_of(x * BY, BY), BY)
            for f in range(4):
                t = tend[f] - E[f - 1, to, :] if f else tend[f]
                final[f, to, :] = 0.5 * (
                    state[f, at, :] + state_p[f, at, :] + ape_time_step * t
                )

        planes(0, BX, 2, correct)
        for c in tables + relays + [a1_left, a1_right, a2_left, a2_right]:
            c.wait_send()
        for c in (a2_left_p, a2_right_p):
            c.wait_send()
        for pair in (edge_prev, edge_pred, late_pred):
            exchange(*pair, "wait_send")
        for lows, highs in ((a1_low, a1_high), (a2_low, a2_high)):
            for low, high in zip(lows, highs):
                exchange(low, high, "wait_send")


def on_device(flow_state, block_offset, block_weight):
    gx_size, gy_size = lax.axis_size("gx"), lax.axis_size("gy")

    def vmem(*shape):
        return pltpu.VMEM(shape, f32)

    def planes_of(fields, count):
        return vmem(fields, count * BY, NZ)

    scratch = [
        planes_of(4, BX + 2),
        *[vmem(4, BX, NZ)] * 4,
        planes_of(4, BX + 2),
        *[vmem(4, BX, NZ)] * 4,
        planes_of(4, BX + 2 * H),
        vmem(2, BX, 3 * BY, NZ),
        planes_of(3, 3 * BX),
        *[vmem(3, 3 * BX, NZ)] * 2,
        planes_of(3, 3 * BX),
        *[vmem(3, 3 * BX, NZ)] * 4,
        planes_of(3, 3 * BX),
        planes_of(3, 3 * BX),
        planes_of(4, BX),
        planes_of(4, BX + 2 * H),
        vmem(2, BX, 3 * BY, NZ),
        planes_of(3, BX),
        planes_of(3, BX),
        vmem(3, BY, NZ),
        vmem(25, BY, NZ),
        pltpu.SMEM((NB,), jnp.int32),
        pltpu.SMEM((NB,), f32),
        pltpu.SemaphoreType.DMA((N_REMOTE,)),
        pltpu.SemaphoreType.DMA((N_REMOTE,)),
        pltpu.SemaphoreType.DMA((N_LOCAL,)),
    ]
    anywhere = pl.BlockSpec(memory_space=pltpu.HBM)
    advanced = pl.pallas_call(
        functools.partial(kernel, gx_size, gy_size),
        out_shape=jax.ShapeDtypeStruct((4, BX * BY, NZ), f32),
        in_specs=[anywhere] * 4,
        out_specs=pl.BlockSpec(memory_space=pltpu.VMEM),
        scratch_shapes=scratch,
        compiler_params=pltpu.CompilerParams(collective_id=0, has_side_effects=True, vmem_limit_bytes=56250000),
        name="heun",
    )(flow_state.reshape(4, BX * BY, NZ), flow_state[0], block_offset, block_weight)
    return advanced.reshape(flow_state.shape)


def solution(mesh):
    placed = (P("grp", None, "gx", "gy", None), P("gx"), P("gx"))
    return jax.shard_map(
        on_device,
        mesh=mesh,
        in_specs=placed,
        out_specs=P("grp", None, "gx", "gy", None),
        check_vma=False,
    )
```

```python
import functools

import jax
import jax.numpy as jnp
from jax import lax
from jax.experimental import pallas as pl
from jax.experimental.pallas import tpu as pltpu
from jax.sharding import PartitionSpec as P

drp_weights = (
    0.907646591371,
    -0.337048393268,
    0.133442885327,
    -0.045246480208,
    0.011169294114,
    -0.001456501759,
)
viscosity = 0.05
mean_flow = 0.5
les_time_step = 0.1
ape_time_step = 0.4

MESH = pl.DeviceIdType.MESH
f32 = jnp.float32

BX = 16
BY = 8
NB = 4
BC = BX // NB
NZ = 128
H = 6

(
    LES_XL, LES_XR, LES_YL, LES_YH,
    PRED_XL, PRED_XR, PRED_YL, PRED_YH,
    RAW_0, RAW_1, RAW_NEXT,
    RELAY_0, RELAY_1,
    TAB_L, TAB_R,
    A1_XL, A1_XR, A1_YLP, A1_YLV, A1_YHP, A1_YHV,
    A2_XL, A2_XR, A2_XLP, A2_XRP, A2_YLP, A2_YLV, A2_YHP, A2_YHV,
    EDGE_NEXT_L, EDGE_NEXT_H,
    OWN_1_L, OWN_1_H, OWN_2_L, OWN_2_H, PREV_1_L, PREV_1_H, PREV_2_L, PREV_2_H,
    EDGE_P_L, EDGE_P_H, LATE_P_L, LATE_P_H,
    N_REMOTE,
) = range(44)
L_FLOW, L_YP, L_YV, L_OFF, L_WT, L_OUT, N_LOCAL = range(7)


def sublane():
    return lax.broadcasted_iota(jnp.int32, (BY, NZ), 0)


def cells_of(first, count):
    return pl.ds(first * BY, count * BY)


def row(ref, f, p):
    return jnp.broadcast_to(ref[f, pl.ds(p, 1), :], (BY, NZ))


def around(cells, low, high, f, plane, edge):
    base = pl.multiple_of(plane * BY, BY)
    centre = cells[f, pl.ds(base, BY), :]
    x_m = cells[f, pl.ds(base - BY, BY), :]
    x_p = cells[f, pl.ds(base + BY, BY), :]
    sub = sublane()
    y_m = jnp.where(sub == 0, row(low, f, edge), pltpu.roll(centre, 1, 0))
    y_p = jnp.where(sub == BY - 1, row(high, f, edge), pltpu.roll(centre, BY - 1, 0))
    z_m = pltpu.roll(centre, 1, 1)
    z_p = pltpu.roll(centre, NZ - 1, 1)
    return centre, x_m, x_p, y_m, y_p, z_m, z_p


def lamb_of(near):
    grad = [
        [0.5 * (n[2] - n[1]), 0.5 * (n[4] - n[3]), 0.5 * (n[6] - n[5])] for n in near[:3]
    ]
    u, v, w = near[0][0], near[1][0], near[2][0]
    vort_x = grad[2][1] - grad[1][2]
    vort_y = grad[0][2] - grad[2][0]
    vort_z = grad[1][0] - grad[0][1]
    lamb = (vort_y * w - vort_z * v, vort_z * u - vort_x * w, vort_x * v - vort_y * u)
    return lamb


def spread_of(n):
    return -6.0 * n[0] + n[2] + n[1] + n[4] + n[3] + n[6] + n[5]


def les_tendency(near):
    lamb = lamb_of(near)
    tend = [-lamb[f] + viscosity * spread_of(near[f]) for f in range(3)]
    if len(near) == 4:
        n = near[3]
        carried = (
            near[0][0] * (0.5 * (n[2] - n[1]))
            + near[1][0] * (0.5 * (n[4] - n[3]))
            + near[2][0] * (0.5 * (n[6] - n[5]))
        )
        tend.append(-carried + viscosity * spread_of(n))
    return tend, lamb


def planes(first, last, unroll, body):
    count = last - first
    assert count % unroll == 0

    def step(i, carry):
        for k in range(unroll):
            body(first + i * unroll + k)
        return carry

    lax.fori_loop(0, count // unroll, step, 0)


def kernel(
    gx_size, gy_size,
    flow, flow_planes, offset, weight, out,
    X, XL, XH, EL, EH, XP, PL, PH, QL, QH,
    F, YE, R, RL, RH, SL, SH, V, VL, VH, WL, WH, LB, LC, G, FP, YP, E, TAB, COEF,
    off_s, wt_s, send_sem, recv_sem, local_sem,
):
    grp, gx, gy = lax.axis_index("grp"), lax.axis_index("gx"), lax.axis_index("gy")
    right = lax.rem(gx + 1, gx_size)
    left = lax.rem(gx + gx_size - 1, gx_size)
    has_low, has_high = gy > 0, gy < gy_size - 1
    is_les, is_ape = grp == 0, grp == 1

    def copy(kind, src, dst, device):
        return pltpu.make_async_remote_copy(
            src_ref=src,
            dst_ref=dst,
            send_sem=send_sem.at[kind],
            recv_sem=recv_sem.at[kind],
            device_id=device,
            device_id_type=MESH,
        )

    def here(kind, src, dst):
        return pltpu.make_async_copy(src, dst, local_sem.at[kind])

    me_left, me_right = (grp, left, gy), (grp, right, gy)
    me_low, me_high = (grp, gx, gy - 1), (grp, gx, gy + 1)

    les_first = [
        copy(LES_XL, flow.at[:, cells_of(0, 1)], X.at[:, cells_of(BX + 1, 1)], me_left),
        copy(LES_XR, flow.at[:, cells_of(BX - 1, 1)], X.at[:, cells_of(0, 1)], me_right),
    ]
    pieces = [(3, 13), (0, 3)]
    velocity = pl.ds(0, 3)
    les_raw = [
        copy(
            RAW_0 + k,
            flow.at[velocity, cells_of(first, count)],
            R.at[:, cells_of(BX + first, count)],
            (1, gx, gy),
        )
        for k, (first, count) in enumerate(pieces)
    ]
    les_next = copy(
        RAW_NEXT, flow.at[velocity, cells_of(0, 14)], R.at[:, cells_of(2 * BX, 14)], (1, left, gy)
    )
    les_edge_low = copy(LES_YL, EL, XH, me_low)
    les_edge_high = copy(LES_YH, EH, XL, me_high)
    pred_x = [
        copy(PRED_XL, XP.at[:, cells_of(1, 1)], XP.at[:, cells_of(BX + 1, 1)], me_left),
        copy(PRED_XR, XP.at[:, cells_of(BX, 1)], XP.at[:, cells_of(0, 1)], me_right),
    ]
    pred_low = copy(PRED_YL, QL, PH, me_low)
    pred_high = copy(PRED_YH, QH, PL, me_high)

    relays = []
    for k, (first, count) in enumerate(pieces):
        start = max(first, 2)
        count = first + count - start
        relays.append(
            copy(
                RELAY_0 + k,
                R.at[:, cells_of(BX + start, count)],
                R.at[:, cells_of(start, count)],
                me_right,
            )
        )
    tables = [
        copy(TAB_L, TAB.at[1], TAB.at[2], me_left),
        copy(TAB_R, TAB.at[1], TAB.at[0], me_right),
    ]
    a1_left = copy(A1_XL, flow.at[:, cells_of(0, H)], F.at[:, cells_of(BX + H, H)], me_left)
    a1_right = copy(A1_XR, flow.at[:, cells_of(BX - H, H)], F.at[:, cells_of(0, H)], me_right)
    low_part, own_part, high_part = pl.ds(0, BY), pl.ds(BY, BY), pl.ds(2 * BY, BY)
    a1_low = [
        copy(A1_YLP, flow_planes.at[0], YE.at[0, :, high_part], me_low),
        copy(A1_YLV, flow_planes.at[2], YE.at[1, :, high_part], me_low),
    ]
    a1_high = [
        copy(A1_YHP, flow_planes.at[0], YE.at[0, :, low_part], me_high),
        copy(A1_YHV, flow_planes.at[2], YE.at[1, :, low_part], me_high),
    ]
    own = cells_of(H, BX)
    flows = pl.ds(1, 3)
    a2_left = copy(A2_XL, FP.at[flows, cells_of(H, H)], FP.at[flows, cells_of(BX + H, H)], me_left)
    a2_right = copy(A2_XR, FP.at[flows, cells_of(BX, H)], FP.at[flows, cells_of(0, H)], me_right)
    a2_left_p = copy(A2_XLP, FP.at[0, cells_of(H, H)], FP.at[0, cells_of(BX + H, H)], me_left)
    a2_right_p = copy(A2_XRP, FP.at[0, cells_of(BX, H)], FP.at[0, cells_of(0, H)], me_right)
    a2_low = [
        copy(A2_YLP, YP.at[0, :, own_part], YP.at[0, :, high_part], me_low),
        copy(A2_YLV, YP.at[1, :, own_part], YP.at[1, :, high_part], me_low),
    ]
    a2_high = [
        copy(A2_YHP, YP.at[0, :, own_part], YP.at[0, :, low_part], me_high),
        copy(A2_YHV, YP.at[1, :, own_part], YP.at[1, :, low_part], me_high),
    ]
    third = [pl.ds(0, BX), pl.ds(BX, BX), pl.ds(2 * BX, BX)]

    edge_next = (
        copy(EDGE_NEXT_L, EL.at[velocity], RH.at[:, third[2]], (1, left, gy - 1)),
        copy(EDGE_NEXT_H, EH.at[velocity], RL.at[:, third[2]], (1, left, gy + 1)),
    )

    def edges(kind, first):
        part = pl.ds(first, 8)
        return (
            copy(kind, SL.at[:, part], RH.at[:, part], me_low),
            copy(kind + 1, SH.at[:, part], RL.at[:, part], me_high),
        )

    edge_own_1, edge_own_2 = edges(OWN_1_L, BX + 8), edges(OWN_2_L, BX)
    edge_prev_1, edge_prev_2 = edges(PREV_1_L, 8), edges(PREV_2_L, 0)
    soon, late = pl.ds(BX, 2 * BX), pl.ds(0, BX)
    edge_pred = (
        copy(EDGE_P_L, WL.at[:, soon], VH.at[:, soon], me_low),
        copy(EDGE_P_H, WH.at[:, soon], VL.at[:, soon], me_high),
    )
    late_pred = (
        copy(LATE_P_L, WL.at[:, late], VH.at[:, late], me_low),
        copy(LATE_P_H, WH.at[:, late], VL.at[:, late], me_high),
    )

    @pl.when(is_les)
    def _():
        here(L_FLOW, flow, X.at[:, cells_of(1, BX)]).start()

    @pl.when(is_ape)
    def _():
        here(L_FLOW, flow, F.at[:, own]).start()
        here(L_YP, flow_planes.at[0], YE.at[0, :, own_part]).start()
        here(L_YV, flow_planes.at[2], YE.at[1, :, own_part]).start()
        here(L_OFF, offset, off_s).start()
        here(L_WT, weight, wt_s).start()

    barrier = pltpu.get_barrier_semaphore()

    def greet(device):
        pl.semaphore_signal(barrier, inc=1, device_id=device, device_id_type=MESH)

    greet(me_left)
    greet(me_right)
    greet((1 - grp, gx, gy))

    @pl.when(is_les)
    def _():
        greet((1, left, gy))

        @pl.when(has_low)
        def _():
            greet((1, left, gy - 1))

        @pl.when(has_high)
        def _():
            greet((1, left, gy + 1))

    @pl.when(is_ape)
    def _():
        greet((0, right, gy))

        @pl.when(has_low)
        def _():
            greet((0, right, gy - 1))

        @pl.when(has_high)
        def _():
            greet((0, right, gy + 1))

    @pl.when(has_low)
    def _():
        greet(me_low)

    @pl.when(has_high)
    def _():
        greet(me_high)

    zeros_edge = jnp.zeros((48, NZ), f32)

    @pl.when(jnp.logical_not(has_low))
    def _():
        for f in range(4):
            XL[f] = zeros_edge[:BX]
            PL[f] = zeros_edge[:BX]
        for f in range(3):
            RL[f] = zeros_edge
            VL[f] = zeros_edge
        for f in range(2):
            YE[f, :, pl.ds(0, BY)] = jnp.zeros((BX, BY, NZ), f32)
            YP[f, :, pl.ds(0, BY)] = jnp.zeros((BX, BY, NZ), f32)

    @pl.when(jnp.logical_not(has_high))
    def _():
        for f in range(4):
            XH[f] = zeros_edge[:BX]
            PH[f] = zeros_edge[:BX]
        for f in range(3):
            RH[f] = zeros_edge
            VH[f] = zeros_edge
        for f in range(2):
            YE[f, :, pl.ds(2 * BY, BY)] = jnp.zeros((BX, BY, NZ), f32)
            YP[f, :, pl.ds(2 * BY, BY)] = jnp.zeros((BX, BY, NZ), f32)

    y_neighbours = jnp.where(has_low, 1, 0) + jnp.where(has_high, 1, 0)

    def exchange(low, high, what):
        @pl.when(has_low)
        def _():
            getattr(low, what)()

        @pl.when(has_high)
        def _():
            getattr(high, what)()

    def pack(cells, first, count, low, high, at, fields):
        for f in range(fields):
            low[f, pl.ds(at, count), :] = cells[f, pl.ds(first * BY, count, stride=BY), :]
            high[f, pl.ds(at, count), :] = cells[
                f, pl.ds(first * BY + BY - 1, count, stride=BY), :
            ]

    @pl.when(is_les)
    def les():
        cells, ahead, final = X, XP, out
        here(L_FLOW, flow, X.at[:, cells_of(1, BX)]).wait()
        pack(cells, 1, BX, EL, EH, 0, 4)
        pl.semaphore_wait(barrier, 4 + 2 * y_neighbours)
        exchange(*edge_next, "start")
        for c in les_raw[:1] + [les_next] + les_first + les_raw[1:]:
            c.start()
        exchange(les_edge_low, les_edge_high, "start")
        for c in les_first:
            c.wait_recv()
        exchange(les_edge_high, les_edge_low, "wait_recv")

        def predict(x):
            near = [around(cells, XL, XH, f, x + 1, x) for f in range(4)]
            tend, _ = les_tendency(near)
            for f in range(4):
                ahead[f, pl.ds(pl.multiple_of((x + 1) * BY, BY), BY), :] = (
                    near[f][0] + les_time_step * tend[f]
                )

        planes(0, BX, 2, predict)
        for c in pred_x:
            c.start()
        pack(ahead, 1, BX, QL, QH, 0, 4)
        exchange(pred_low, pred_high, "start")
        for c in pred_x:
            c.wait_recv()
        exchange(pred_high, pred_low, "wait_recv")

        def correct(x):
            near = [around(ahead, PL, PH, f, x + 1, x) for f in range(4)]
            tend, _ = les_tendency(near)
            for f in range(4):
                before = cells[f, pl.ds(pl.multiple_of((x + 1) * BY, BY), BY), :]
                final[f, pl.ds(pl.multiple_of(x * BY, BY), BY), :] = 0.5 * (
                    before + near[f][0] + les_time_step * tend[f]
                )

        planes(0, BX, 2, correct)
        for c in les_raw + [les_next] + les_first + pred_x:
            c.wait_send()
        exchange(les_edge_low, les_edge_high, "wait_send")
        exchange(pred_low, pred_high, "wait_send")
        exchange(*edge_next, "wait_send")

    @pl.when(is_ape)
    def ape():
        raw, state, ahead, rate, state_p, final = R, F, V, G, FP, out

        here(L_OFF, offset, off_s).wait()
        here(L_WT, weight, wt_s).wait()
        sub = sublane()
        table = jnp.zeros((BY, NZ), f32)
        for b in range(NB):
            table = jnp.where(sub == b, off_s[b].astype(f32), table)
            table = jnp.where(sub == NB + b, wt_s[b], table)
        TAB[1] = table

        pl.semaphore_wait(barrier, 4 + 2 * y_neighbours)
        for c in tables:
            c.start()
        a1_left.start()
        for low, high in zip(a1_low, a1_high):
            exchange(low, high, "start")

        def thirteen(plus, minus):
            total = None
            for j, c in enumerate(drp_weights, start=1):
                term = c * (plus(j) - minus(j))
                total = term if total is None else total + term
            return total

        def rate_z(cells):
            def body(x):
                at = pl.multiple_of((x + H) * BY, BY)
                to = pl.ds(pl.multiple_of(x * BY, BY), BY)
                p, w = cells[0, pl.ds(at, BY), :], cells[3, pl.ds(at, BY), :]
                dz = [
                    thirteen(lambda j: pltpu.roll(q, NZ - j, 1), lambda j: pltpu.roll(q, j, 1))
                    for q in (p, w)
                ]
                rate[0, to, :] = -dz[1]
                rate[3, to, :] = -dz[0]

            planes(0, BX, 2, body)

        def rate_y(walls):
            def body(x):
                to = pl.ds(pl.multiple_of(x * BY, BY), BY)
                dy = [
                    thirteen(
                        lambda j: walls[f, x, pl.ds(BY + j, BY), :],
                        lambda j: walls[f, x, pl.ds(BY - j, BY), :],
                    )
                    for f in range(2)
                ]
                rate[0, to, :] = rate[0, to, :] - dy[1]
                rate[2, to, :] = -dy[0]

            planes(0, BX, 2, body)

        def rate_x(cells, x):
            at = (x + H) * BY

            def along(f):
                return thirteen(
                    lambda j: cells[f, pl.ds(pl.multiple_of(at + j * BY, BY), BY), :],
                    lambda j: cells[f, pl.ds(pl.multiple_of(at - j * BY, BY), BY), :],
                )

            to = pl.ds(pl.multiple_of(x * BY, BY), BY)
            dx = [along(f) for f in range(4)]
            return (
                rate[0, to, :] - mean_flow * dx[0] - dx[1],
                -mean_flow * dx[1] - dx[0],
                rate[2, to, :] - mean_flow * dx[2],
                rate[3, to, :] - mean_flow * dx[3],
            )

        here(L_FLOW, flow, F.at[:, own]).wait()
        rate_z(state)

        pairs = []
        for d in range(NB):
            for part, shift in enumerate((NB, 0, -NB)):
                for b in range(NB):
                    near_block, far_block = 1 - NB, NB
                    lowest = b + (near_block if b < NB - 1 else 0)
                    highest = b + (far_block if b > 0 else 0)
                    if lowest <= d + shift <= highest:
                        pairs.append((d, part, b, d + shift))

        def first_lamb(p):
            near = [around(raw, RL, RH, f, p, p) for f in range(3)]
            tend, lamb = les_tendency(near)
            to = pl.ds(pl.multiple_of(p * BY, BY), BY)
            for f in range(3):
                ahead[f, to, :] = near[f][0] + les_time_step * tend[f]
                LB[f, to, :] = lamb[f]

        def second_lamb(p):
            near = [around(ahead, VL, VH, f, p, p - 1) for f in range(3)]
            lamb = lamb_of(near)
            to = pl.ds(pl.multiple_of(p * BY, BY), BY)
            for f in range(3):
                LC[f, to, :] = lamb[f]

        def deposit(moved, is_late, add):
            for d in range(NB):
                terms = [
                    (k, part * BX + b * BC)
                    for k, (to, part, b, _) in enumerate(pairs)
                    if to == d and is_late == (part * NB + b <= NB)
                ]

                def body(r, carry):
                    for f in range(3):
                        total = None
                        for k, first in terms:
                            at = pl.multiple_of((first + r) * BY, BY)
                            term = COEF[k] * moved[f, pl.ds(at, BY), :]
                            total = term if total is None else total + term
                        add(f, d * BC + r, total)
                    return carry

                lax.fori_loop(0, BC, body, 0)

        def keep_in(ref):
            def add(f, x, total):
                ref[f, pl.ds(pl.multiple_of(x * BY, BY), BY), :] = total

            return add

        les_raw[0].wait_recv()
        relays[0].start()
        a1_right.start()
        pack(raw, BX + 8, 8, SL, SH, BX + 8, 3)
        exchange(*edge_own_1, "start")
        les_raw[1].wait_recv()
        relays[1].start()
        pack(raw, BX, 8, SL, SH, BX, 3)
        exchange(*edge_own_2, "start")

        exchange(edge_next[1], edge_next[0], "wait_recv")
        les_next.wait_recv()
        exchange(edge_own_1[1], edge_own_1[0], "wait_recv")
        planes(BX + 9, 2 * BX + 13, 2, first_lamb)
        for c in tables:
            c.wait_recv()
        for k, (d, part, b, aim) in enumerate(pairs):
            target = row(TAB, part, b) + float(b)
            share = row(TAB, part, NB + b)
            COEF[k] = jnp.where(target == float(aim), share, 0.0) + jnp.where(
                target + 1.0 == float(aim), 1.0 - share, 0.0
            )

        here(L_YP, flow_planes.at[0], YE.at[0, :, own_part]).wait()
        here(L_YV, flow_planes.at[2], YE.at[1, :, own_part]).wait()
        for low, high in zip(a1_low, a1_high):
            exchange(high, low, "wait_recv")
        rate_y(YE)

        relays[0].wait_recv()
        pack(raw, 8, 8, SL, SH, 8, 3)
        exchange(*edge_prev_1, "start")
        pack(raw, 3, 5, SL, SH, 3, 3)
        exchange(*edge_prev_2, "start")

        a1_left.wait_recv()
        a1_right.wait_recv()

        def predict(x):
            tend = rate_x(state, x)
            at = pl.ds(pl.multiple_of((x + H) * BY, BY), BY)
            for f in range(4):
                predicted = state[f, at, :] + ape_time_step * tend[f]
                state_p[f, at, :] = predicted
                if f == 0:
                    YP[0, x, own_part, :] = predicted

        planes(0, BX, 2, predict)
        a2_left_p.start()
        a2_right_p.start()
        exchange(a2_low[0], a2_high[0], "start")

        def take_part(f, x, total):
            at = pl.ds(pl.multiple_of((x + H) * BY, BY), BY)
            state_p[f + 1, at, :] = state_p[f + 1, at, :] - ape_time_step * total

        exchange(edge_own_2[1], edge_own_2[0], "wait_recv")
        planes(BX + 1, BX + 9, 2, first_lamb)
        pack(ahead, BX + 1, 28, WL, WH, BX, 3)
        exchange(*edge_pred, "start")
        deposit(LB, False, take_part)

        exchange(edge_prev_1[1], edge_prev_1[0], "wait_recv")
        planes(9, BX + 1, 2, first_lamb)
        exchange(edge_prev_2[1], edge_prev_2[0], "wait_recv")
        planes(4, 8, 2, first_lamb)
        planes(8, 9, 1, first_lamb)

        def take_source(f, x, total):
            at = pl.ds(pl.multiple_of((x + H) * BY, BY), BY)
            predicted = state_p[f + 1, at, :] - ape_time_step * total
            state_p[f + 1, at, :] = predicted
            if f == 1:
                YP[1, x, own_part, :] = predicted

        deposit(LB, True, take_source)
        a2_left.start()
        a2_right.start()
        exchange(a2_low[1], a2_high[1], "start")
        pack(ahead, 1, BX, WL, WH, 0, 3)
        exchange(*late_pred, "start")
        relays[1].wait_recv()
        planes(3, 4, 1, first_lamb)

        rate_z(state_p)
        exchange(edge_pred[1], edge_pred[0], "wait_recv")
        planes(BX + 2, BX + 28, 2, second_lamb)
        deposit(LC, False, keep_in(E))
        for low, high in zip(a2_low, a2_high):
            exchange(high, low, "wait_recv")
        rate_y(YP)

        def more_source(f, x, total):
            to = pl.ds(pl.multiple_of(x * BY, BY), BY)
            E[f, to, :] = E[f, to, :] + total

        exchange(late_pred[1], late_pred[0], "wait_recv")
        planes(4, BX + 2, 2, second_lamb)
        deposit(LC, True, more_source)
        for c in (a2_left_p, a2_right_p, a2_left, a2_right):
            c.wait_recv()

        def correct(x):
            tend = rate_x(state_p, x)
            at = pl.ds(pl.multiple_of((x + H) * BY, BY), BY)
            to = pl.ds(pl.multiple_of(x * BY, BY), BY)
            for f in range(4):
                t = tend[f] - E[f - 1, to, :] if f else tend[f]
                final[f, to, :] = 0.5 * (
                    state[f, at, :] + state_p[f, at, :] + ape_time_step * t
                )

        planes(0, BX, 2, correct)
        for c in tables + relays + [a1_left, a1_right, a2_left, a2_right]:
            c.wait_send()
        for c in (a2_left_p, a2_right_p):
            c.wait_send()
        for pair in (edge_own_1, edge_own_2, edge_prev_1, edge_prev_2, edge_pred, late_pred):
            exchange(*pair, "wait_send")
        for lows, highs in ((a1_low, a1_high), (a2_low, a2_high)):
            for low, high in zip(lows, highs):
                exchange(low, high, "wait_send")


def on_device(flow_state, block_offset, block_weight):
    gx_size, gy_size = lax.axis_size("gx"), lax.axis_size("gy")

    def vmem(*shape):
        return pltpu.VMEM(shape, f32)

    def planes_of(fields, count):
        return vmem(fields, count * BY, NZ)

    scratch = [
        planes_of(4, BX + 2),
        *[vmem(4, BX, NZ)] * 4,
        planes_of(4, BX + 2),
        *[vmem(4, BX, NZ)] * 4,
        planes_of(4, BX + 2 * H),
        vmem(2, BX, 3 * BY, NZ),
        planes_of(3, 3 * BX),
        *[vmem(3, 3 * BX, NZ)] * 2,
        *[vmem(3, 2 * BX, NZ)] * 2,
        planes_of(3, 3 * BX),
        *[vmem(3, 3 * BX, NZ)] * 4,
        planes_of(3, 3 * BX),
        planes_of(3, 3 * BX),
        planes_of(4, BX),
        planes_of(4, BX + 2 * H),
        vmem(2, BX, 3 * BY, NZ),
        planes_of(3, BX),
        vmem(3, BY, NZ),
        vmem(25, BY, NZ),
        pltpu.SMEM((NB,), jnp.int32),
        pltpu.SMEM((NB,), f32),
        pltpu.SemaphoreType.DMA((N_REMOTE,)),
        pltpu.SemaphoreType.DMA((N_REMOTE,)),
        pltpu.SemaphoreType.DMA((N_LOCAL,)),
    ]
    anywhere = pl.BlockSpec(memory_space=pltpu.HBM)
    advanced = pl.pallas_call(
        functools.partial(kernel, gx_size, gy_size),
        out_shape=jax.ShapeDtypeStruct((4, BX * BY, NZ), f32),
        in_specs=[anywhere] * 4,
        out_specs=pl.BlockSpec(memory_space=pltpu.VMEM),
        scratch_shapes=scratch,
        compiler_params=pltpu.CompilerParams(collective_id=0, has_side_effects=True, vmem_limit_bytes=56250000),
        name="heun",
    )(flow_state.reshape(4, BX * BY, NZ), flow_state[0], block_offset, block_weight)
    return advanced.reshape(flow_state.shape)


def solution(mesh):
    placed = (P("grp", None, "gx", "gy", None), P("gx"), P("gx"))
    return jax.shard_map(
        on_device,
        mesh=mesh,
        in_specs=placed,
        out_specs=P("grp", None, "gx", "gy", None),
        check_vma=False,
    )
```

```python
import functools

import jax
import jax.numpy as jnp
from jax import lax
from jax.experimental import pallas as pl
from jax.experimental.pallas import tpu as pltpu
from jax.sharding import PartitionSpec as P

drp_weights = (
    0.907646591371,
    -0.337048393268,
    0.133442885327,
    -0.045246480208,
    0.011169294114,
    -0.001456501759,
)
viscosity = 0.05
mean_flow = 0.5
les_time_step = 0.1
ape_time_step = 0.4

MESH = pl.DeviceIdType.MESH
f32 = jnp.float32

BX = 16
BY = 8
NB = 4
BC = BX // NB
NZ = 128
H = 6

(
    LES_XL, LES_XR, LES_YL, LES_YH,
    PRED_XL, PRED_XR, PRED_YL, PRED_YH,
    RAW_0, RAW_1, RAW_NEXT,
    RELAY_0, RELAY_1,
    TAB_L, TAB_R,
    A1_XL, A1_XR, A1_YLP, A1_YLV, A1_YHP, A1_YHV,
    A2_XL, A2_XR, A2_XLP, A2_XRP, A2_YLP, A2_YLV, A2_YHP, A2_YHV,
    EDGE_NEXT_L, EDGE_NEXT_H,
    OWN_1_L, OWN_1_H, OWN_2_L, OWN_2_H, PREV_1_L, PREV_1_H, PREV_2_L, PREV_2_H,
    EDGE_P_L, EDGE_P_H, LATE_P_L, LATE_P_H,
    N_REMOTE,
) = range(44)
L_FLOW, L_YP, L_YV, L_OFF, L_WT, L_OUT, N_LOCAL = range(7)


def sublane():
    return lax.broadcasted_iota(jnp.int32, (BY, NZ), 0)


def cells_of(first, count):
    return pl.ds(first * BY, count * BY)


def row(ref, f, p):
    return jnp.broadcast_to(ref[f, pl.ds(p, 1), :], (BY, NZ))


def around(cells, low, high, f, plane, edge):
    base = pl.multiple_of(plane * BY, BY)
    centre = cells[f, pl.ds(base, BY), :]
    x_m = cells[f, pl.ds(base - BY, BY), :]
    x_p = cells[f, pl.ds(base + BY, BY), :]
    sub = sublane()
    y_m = jnp.where(sub == 0, row(low, f, edge), pltpu.roll(centre, 1, 0))
    y_p = jnp.where(sub == BY - 1, row(high, f, edge), pltpu.roll(centre, BY - 1, 0))
    z_m = pltpu.roll(centre, 1, 1)
    z_p = pltpu.roll(centre, NZ - 1, 1)
    return centre, x_m, x_p, y_m, y_p, z_m, z_p


def lamb_of(near):
    grad = [
        [0.5 * (n[2] - n[1]), 0.5 * (n[4] - n[3]), 0.5 * (n[6] - n[5])] for n in near[:3]
    ]
    u, v, w = near[0][0], near[1][0], near[2][0]
    vort_x = grad[2][1] - grad[1][2]
    vort_y = grad[0][2] - grad[2][0]
    vort_z = grad[1][0] - grad[0][1]
    lamb = (vort_y * w - vort_z * v, vort_z * u - vort_x * w, vort_x * v - vort_y * u)
    return lamb


def spread_of(n):
    return -6.0 * n[0] + n[2] + n[1] + n[4] + n[3] + n[6] + n[5]


def les_tendency(near):
    lamb = lamb_of(near)
    tend = [-lamb[f] + viscosity * spread_of(near[f]) for f in range(3)]
    if len(near) == 4:
        n = near[3]
        carried = (
            near[0][0] * (0.5 * (n[2] - n[1]))
            + near[1][0] * (0.5 * (n[4] - n[3]))
            + near[2][0] * (0.5 * (n[6] - n[5]))
        )
        tend.append(-carried + viscosity * spread_of(n))
    return tend, lamb


def planes(first, last, unroll, body):
    count = last - first
    assert count % unroll == 0

    def step(i, carry):
        for k in range(unroll):
            body(first + i * unroll + k)
        return carry

    lax.fori_loop(0, count // unroll, step, 0)


def kernel(
    gx_size, gy_size,
    flow, flow_planes, offset, weight, out,
    X, XL, XH, EL, EH, XP, PL, PH, QL, QH,
    F, YE, R, RL, RH, SL, SH, V, VL, VH, WL, WH, LB, LC, G, FP, YP, D, E, TAB, COEF,
    off_s, wt_s, send_sem, recv_sem, local_sem,
):
    grp, gx, gy = lax.axis_index("grp"), lax.axis_index("gx"), lax.axis_index("gy")
    right = lax.rem(gx + 1, gx_size)
    left = lax.rem(gx + gx_size - 1, gx_size)
    has_low, has_high = gy > 0, gy < gy_size - 1
    is_les, is_ape = grp == 0, grp == 1
    place = lax.rem(gx, 4)

    def copy(kind, src, dst, device):
        return pltpu.make_async_remote_copy(
            src_ref=src,
            dst_ref=dst,
            send_sem=send_sem.at[kind],
            recv_sem=recv_sem.at[kind],
            device_id=device,
            device_id_type=MESH,
        )

    def here(kind, src, dst):
        return pltpu.make_async_copy(src, dst, local_sem.at[kind])

    me_left, me_right = (grp, left, gy), (grp, right, gy)
    me_low, me_high = (grp, gx, gy - 1), (grp, gx, gy + 1)

    les_first = [
        copy(LES_XL, flow.at[:, cells_of(0, 1)], X.at[:, cells_of(BX + 1, 1)], me_left),
        copy(LES_XR, flow.at[:, cells_of(BX - 1, 1)], X.at[:, cells_of(0, 1)], me_right),
    ]
    pieces = [(3, 13), (0, 3)]
    velocity = pl.ds(0, 3)
    les_raw = [
        copy(
            RAW_0 + k,
            flow.at[velocity, cells_of(first, count)],
            R.at[:, cells_of(BX + first, count)],
            (1, gx, gy),
        )
        for k, (first, count) in enumerate(pieces)
    ]
    les_next = copy(
        RAW_NEXT, flow.at[velocity, cells_of(0, 14)], R.at[:, cells_of(2 * BX, 14)], (1, left, gy)
    )
    les_edge_low = copy(LES_YL, EL, XH, me_low)
    les_edge_high = copy(LES_YH, EH, XL, me_high)
    pred_x = [
        copy(PRED_XL, XP.at[:, cells_of(1, 1)], XP.at[:, cells_of(BX + 1, 1)], me_left),
        copy(PRED_XR, XP.at[:, cells_of(BX, 1)], XP.at[:, cells_of(0, 1)], me_right),
    ]
    pred_low = copy(PRED_YL, QL, PH, me_low)
    pred_high = copy(PRED_YH, QH, PL, me_high)

    relays = []
    for k, (first, count) in enumerate(pieces):
        start = max(first, 2)
        count = first + count - start
        relays.append(
            copy(
                RELAY_0 + k,
                R.at[:, cells_of(BX + start, count)],
                R.at[:, cells_of(start, count)],
                me_right,
            )
        )
    tables = [
        copy(TAB_L, TAB.at[1], TAB.at[2], me_left),
        copy(TAB_R, TAB.at[1], TAB.at[0], me_right),
    ]
    a1_left = copy(A1_XL, flow.at[:, cells_of(0, H)], F.at[:, cells_of(BX + H, H)], me_left)
    a1_right = copy(A1_XR, flow.at[:, cells_of(BX - H, H)], F.at[:, cells_of(0, H)], me_right)
    low_part, own_part, high_part = pl.ds(0, BY), pl.ds(BY, BY), pl.ds(2 * BY, BY)
    a1_low = [
        copy(A1_YLP, flow_planes.at[0], YE.at[0, :, high_part], me_low),
        copy(A1_YLV, flow_planes.at[2], YE.at[1, :, high_part], me_low),
    ]
    a1_high = [
        copy(A1_YHP, flow_planes.at[0], YE.at[0, :, low_part], me_high),
        copy(A1_YHV, flow_planes.at[2], YE.at[1, :, low_part], me_high),
    ]
    own = cells_of(H, BX)
    flows = pl.ds(1, 3)
    a2_left = copy(A2_XL, FP.at[flows, cells_of(H, H)], FP.at[flows, cells_of(BX + H, H)], me_left)
    a2_right = copy(A2_XR, FP.at[flows, cells_of(BX, H)], FP.at[flows, cells_of(0, H)], me_right)
    a2_left_p = copy(A2_XLP, FP.at[0, cells_of(H, H)], FP.at[0, cells_of(BX + H, H)], me_left)
    a2_right_p = copy(A2_XRP, FP.at[0, cells_of(BX, H)], FP.at[0, cells_of(0, H)], me_right)
    a2_low = [
        copy(A2_YLP, YP.at[0, :, own_part], YP.at[0, :, high_part], me_low),
        copy(A2_YLV, YP.at[1, :, own_part], YP.at[1, :, high_part], me_low),
    ]
    a2_high = [
        copy(A2_YHP, YP.at[0, :, own_part], YP.at[0, :, low_part], me_high),
        copy(A2_YHV, YP.at[1, :, own_part], YP.at[1, :, low_part], me_high),
    ]
    third = [pl.ds(0, BX), pl.ds(BX, BX), pl.ds(2 * BX, BX)]

    edge_next = (
        copy(EDGE_NEXT_L, EL.at[velocity], RH.at[:, third[2]], (1, left, gy - 1)),
        copy(EDGE_NEXT_H, EH.at[velocity], RL.at[:, third[2]], (1, left, gy + 1)),
    )

    def edges(kind, first):
        part = pl.ds(first, 8)
        return (
            copy(kind, SL.at[:, part], RH.at[:, part], me_low),
            copy(kind + 1, SH.at[:, part], RL.at[:, part], me_high),
        )

    edge_own_1, edge_own_2 = edges(OWN_1_L, BX + 8), edges(OWN_2_L, BX)
    edge_prev_1, edge_prev_2 = edges(PREV_1_L, 8), edges(PREV_2_L, 0)
    soon, late = pl.ds(BX, 2 * BX), pl.ds(0, BX)
    edge_pred = (
        copy(EDGE_P_L, WL.at[:, soon], VH.at[:, soon], me_low),
        copy(EDGE_P_H, WH.at[:, soon], VL.at[:, soon], me_high),
    )
    late_pred = (
        copy(LATE_P_L, WL.at[:, late], VH.at[:, late], me_low),
        copy(LATE_P_H, WH.at[:, late], VL.at[:, late], me_high),
    )

    @pl.when(is_les)
    def _():
        here(L_FLOW, flow, X.at[:, cells_of(1, BX)]).start()

    @pl.when(is_ape)
    def _():
        here(L_FLOW, flow, F.at[:, own]).start()
        here(L_YP, flow_planes.at[0], YE.at[0, :, own_part]).start()
        here(L_YV, flow_planes.at[2], YE.at[1, :, own_part]).start()
        here(L_OFF, offset, off_s).start()
        here(L_WT, weight, wt_s).start()

    barrier = pltpu.get_barrier_semaphore()

    def greet(device):
        pl.semaphore_signal(barrier, inc=1, device_id=device, device_id_type=MESH)

    greet(me_left)
    greet(me_right)
    greet((1 - grp, gx, gy))

    @pl.when(is_les)
    def _():
        greet((1, left, gy))

        @pl.when(has_low)
        def _():
            greet((1, left, gy - 1))

        @pl.when(has_high)
        def _():
            greet((1, left, gy + 1))

    @pl.when(is_ape)
    def _():
        greet((0, right, gy))

        @pl.when(has_low)
        def _():
            greet((0, right, gy - 1))

        @pl.when(has_high)
        def _():
            greet((0, right, gy + 1))

    @pl.when(has_low)
    def _():
        greet(me_low)

    @pl.when(has_high)
    def _():
        greet(me_high)

    zeros_edge = jnp.zeros((48, NZ), f32)

    @pl.when(jnp.logical_not(has_low))
    def _():
        for f in range(4):
            XL[f] = zeros_edge[:BX]
            PL[f] = zeros_edge[:BX]
        for f in range(3):
            RL[f] = zeros_edge
            VL[f] = zeros_edge
        for f in range(2):
            YE[f, :, pl.ds(0, BY)] = jnp.zeros((BX, BY, NZ), f32)
            YP[f, :, pl.ds(0, BY)] = jnp.zeros((BX, BY, NZ), f32)

    @pl.when(jnp.logical_not(has_high))
    def _():
        for f in range(4):
            XH[f] = zeros_edge[:BX]
            PH[f] = zeros_edge[:BX]
        for f in range(3):
            RH[f] = zeros_edge
            VH[f] = zeros_edge
        for f in range(2):
            YE[f, :, pl.ds(2 * BY, BY)] = jnp.zeros((BX, BY, NZ), f32)
            YP[f, :, pl.ds(2 * BY, BY)] = jnp.zeros((BX, BY, NZ), f32)

    y_neighbours = jnp.where(has_low, 1, 0) + jnp.where(has_high, 1, 0)

    def exchange(low, high, what):
        @pl.when(has_low)
        def _():
            getattr(low, what)()

        @pl.when(has_high)
        def _():
            getattr(high, what)()

    def pack(cells, first, count, low, high, at, fields):
        for f in range(fields):
            low[f, pl.ds(at, count), :] = cells[f, pl.ds(first * BY, count, stride=BY), :]
            high[f, pl.ds(at, count), :] = cells[
                f, pl.ds(first * BY + BY - 1, count, stride=BY), :
            ]

    @pl.when(is_les)
    def les():
        cells, ahead, final = X, XP, out
        here(L_FLOW, flow, X.at[:, cells_of(1, BX)]).wait()
        pack(cells, 1, BX, EL, EH, 0, 4)
        pl.semaphore_wait(barrier, 4 + 2 * y_neighbours)
        exchange(*edge_next, "start")
        for c in les_raw[:1] + [les_next] + les_first + les_raw[1:]:
            c.start()
        exchange(les_edge_low, les_edge_high, "start")
        for c in les_first:
            c.wait_recv()
        exchange(les_edge_high, les_edge_low, "wait_recv")

        def predict(x):
            near = [around(cells, XL, XH, f, x + 1, x) for f in range(4)]
            tend, _ = les_tendency(near)
            for f in range(4):
                ahead[f, pl.ds(pl.multiple_of((x + 1) * BY, BY), BY), :] = (
                    near[f][0] + les_time_step * tend[f]
                )

        planes(0, BX, 2, predict)
        for c in pred_x:
            c.start()
        pack(ahead, 1, BX, QL, QH, 0, 4)
        exchange(pred_low, pred_high, "start")
        for c in pred_x:
            c.wait_recv()
        exchange(pred_high, pred_low, "wait_recv")

        def correct(x):
            near = [around(ahead, PL, PH, f, x + 1, x) for f in range(4)]
            tend, _ = les_tendency(near)
            for f in range(4):
                before = cells[f, pl.ds(pl.multiple_of((x + 1) * BY, BY), BY), :]
                final[f, pl.ds(pl.multiple_of(x * BY, BY), BY), :] = 0.5 * (
                    before + near[f][0] + les_time_step * tend[f]
                )

        planes(0, BX, 2, correct)
        for c in les_raw + [les_next] + les_first + pred_x:
            c.wait_send()
        exchange(les_edge_low, les_edge_high, "wait_send")
        exchange(pred_low, pred_high, "wait_send")
        exchange(*edge_next, "wait_send")

    @pl.when(is_ape)
    def ape():
        raw, state, ahead, rate, state_p, final = R, F, V, G, FP, out

        here(L_OFF, offset, off_s).wait()
        here(L_WT, weight, wt_s).wait()
        sub = sublane()
        table = jnp.zeros((BY, NZ), f32)
        for b in range(NB):
            table = jnp.where(sub == b, off_s[b].astype(f32), table)
            table = jnp.where(sub == NB + b, wt_s[b], table)
        TAB[1] = table

        pl.semaphore_wait(barrier, 4 + 2 * y_neighbours)
        for c in tables:
            c.start()

        @pl.when((place == 0))
        def _():
            a1_right.start()


        @pl.when((place == 1) | (place == 2) | (place == 3))
        def _():
            a1_left.start()

        for low, high in zip(a1_low, a1_high):
            exchange(low, high, "start")

        def thirteen(plus, minus):
            total = None
            for j, c in enumerate(drp_weights, start=1):
                term = c * (plus(j) - minus(j))
                total = term if total is None else total + term
            return total

        def rate_z(cells):
            def body(x):
                at = pl.multiple_of((x + H) * BY, BY)
                to = pl.ds(pl.multiple_of(x * BY, BY), BY)
                p, w = cells[0, pl.ds(at, BY), :], cells[3, pl.ds(at, BY), :]
                dz = [
                    thirteen(lambda j: pltpu.roll(q, NZ - j, 1), lambda j: pltpu.roll(q, j, 1))
                    for q in (p, w)
                ]
                rate[0, to, :] = -dz[1]
                rate[3, to, :] = -dz[0]

            planes(0, BX, 2, body)

        def rate_y(walls):
            def body(x):
                to = pl.ds(pl.multiple_of(x * BY, BY), BY)
                dy = [
                    thirteen(
                        lambda j: walls[f, x, pl.ds(BY + j, BY), :],
                        lambda j: walls[f, x, pl.ds(BY - j, BY), :],
                    )
                    for f in range(2)
                ]
                rate[0, to, :] = rate[0, to, :] - dy[1]
                rate[2, to, :] = -dy[0]

            planes(0, BX, 2, body)

        def rate_x(cells, x):
            at = (x + H) * BY

            def along(f):
                return thirteen(
                    lambda j: cells[f, pl.ds(pl.multiple_of(at + j * BY, BY), BY), :],
                    lambda j: cells[f, pl.ds(pl.multiple_of(at - j * BY, BY), BY), :],
                )

            to = pl.ds(pl.multiple_of(x * BY, BY), BY)
            dx = [along(f) for f in range(4)]
            return (
                rate[0, to, :] - mean_flow * dx[0] - dx[1],
                -mean_flow * dx[1] - dx[0],
                rate[2, to, :] - mean_flow * dx[2],
                rate[3, to, :] - mean_flow * dx[3],
            )

        here(L_FLOW, flow, F.at[:, own]).wait()
        rate_z(state)

        pairs = []
        for d in range(NB):
            for part, shift in enumerate((NB, 0, -NB)):
                for b in range(NB):
                    near_block, far_block = 1 - NB, NB
                    lowest = b + (near_block if b < NB - 1 else 0)
                    highest = b + (far_block if b > 0 else 0)
                    if lowest <= d + shift <= highest:
                        pairs.append((d, part, b, d + shift))

        def first_lamb(p):
            near = [around(raw, RL, RH, f, p, p) for f in range(3)]
            tend, lamb = les_tendency(near)
            to = pl.ds(pl.multiple_of(p * BY, BY), BY)
            for f in range(3):
                ahead[f, to, :] = near[f][0] + les_time_step * tend[f]
                LB[f, to, :] = lamb[f]

        def second_lamb(p):
            near = [around(ahead, VL, VH, f, p, p - 1) for f in range(3)]
            lamb = lamb_of(near)
            to = pl.ds(pl.multiple_of(p * BY, BY), BY)
            for f in range(3):
                LC[f, to, :] = lamb[f]

        def deposit(moved, is_late, add):
            for d in range(NB):
                terms = [
                    (k, part * BX + b * BC)
                    for k, (to, part, b, _) in enumerate(pairs)
                    if to == d and is_late == (part * NB + b <= NB)
                ]

                def body(r, carry):
                    for f in range(3):
                        total = None
                        for k, first in terms:
                            at = pl.multiple_of((first + r) * BY, BY)
                            term = COEF[k] * moved[f, pl.ds(at, BY), :]
                            total = term if total is None else total + term
                        add(f, d * BC + r, total)
                    return carry

                lax.fori_loop(0, BC, body, 0)

        def keep_in(ref):
            def add(f, x, total):
                ref[f, pl.ds(pl.multiple_of(x * BY, BY), BY), :] = total

            return add

        les_raw[0].wait_recv()
        relays[0].start()

        @pl.when((place == 0))
        def _():
            a1_left.start()


        @pl.when((place == 1) | (place == 3))
        def _():
            a1_right.start()

        pack(raw, BX + 8, 8, SL, SH, BX + 8, 3)
        exchange(*edge_own_1, "start")
        les_raw[1].wait_recv()
        relays[1].start()
        pack(raw, BX, 8, SL, SH, BX, 3)
        exchange(*edge_own_2, "start")

        exchange(edge_next[1], edge_next[0], "wait_recv")
        les_next.wait_recv()

        @pl.when((place == 2))
        def _():
            a1_right.start()

        exchange(edge_own_1[1], edge_own_1[0], "wait_recv")
        planes(BX + 9, 2 * BX + 13, 2, first_lamb)
        for c in tables:
            c.wait_recv()
        for k, (d, part, b, aim) in enumerate(pairs):
            target = row(TAB, part, b) + float(b)
            share = row(TAB, part, NB + b)
            COEF[k] = jnp.where(target == float(aim), share, 0.0) + jnp.where(
                target + 1.0 == float(aim), 1.0 - share, 0.0
            )

        here(L_YP, flow_planes.at[0], YE.at[0, :, own_part]).wait()
        here(L_YV, flow_planes.at[2], YE.at[1, :, own_part]).wait()
        for low, high in zip(a1_low, a1_high):
            exchange(high, low, "wait_recv")
        rate_y(YE)

        relays[0].wait_recv()
        pack(raw, 8, 8, SL, SH, 8, 3)
        exchange(*edge_prev_1, "start")
        pack(raw, 3, 5, SL, SH, 3, 3)
        exchange(*edge_prev_2, "start")

        exchange(edge_own_2[1], edge_own_2[0], "wait_recv")
        planes(BX + 1, BX + 9, 2, first_lamb)
        pack(ahead, BX + 1, 28, WL, WH, BX, 3)
        exchange(*edge_pred, "start")
        deposit(LB, False, keep_in(D))

        a1_left.wait_recv()
        a1_right.wait_recv()

        def predict(x):
            tend = rate_x(state, x)
            at = pl.ds(pl.multiple_of((x + H) * BY, BY), BY)
            to = pl.ds(pl.multiple_of(x * BY, BY), BY)
            for f in range(4):
                t = tend[f] - D[f - 1, to, :] if f else tend[f]
                predicted = state[f, at, :] + ape_time_step * t
                state_p[f, at, :] = predicted
                if f == 0:
                    YP[0, x, own_part, :] = predicted

        planes(0, BX, 2, predict)
        a2_left_p.start()
        a2_right_p.start()
        exchange(a2_low[0], a2_high[0], "start")

        exchange(edge_prev_1[1], edge_prev_1[0], "wait_recv")
        planes(9, BX + 1, 2, first_lamb)
        exchange(edge_prev_2[1], edge_prev_2[0], "wait_recv")
        planes(4, 8, 2, first_lamb)
        planes(8, 9, 1, first_lamb)

        def take_source(f, x, total):
            at = pl.ds(pl.multiple_of((x + H) * BY, BY), BY)
            predicted = state_p[f + 1, at, :] - ape_time_step * total
            state_p[f + 1, at, :] = predicted
            if f == 1:
                YP[1, x, own_part, :] = predicted

        deposit(LB, True, take_source)
        a2_left.start()
        a2_right.start()
        exchange(a2_low[1], a2_high[1], "start")
        pack(ahead, 1, BX, WL, WH, 0, 3)
        exchange(*late_pred, "start")
        relays[1].wait_recv()
        planes(3, 4, 1, first_lamb)

        rate_z(state_p)
        exchange(edge_pred[1], edge_pred[0], "wait_recv")
        planes(BX + 2, BX + 28, 2, second_lamb)
        deposit(LC, False, keep_in(E))
        for low, high in zip(a2_low, a2_high):
            exchange(high, low, "wait_recv")
        rate_y(YP)

        def more_source(f, x, total):
            to = pl.ds(pl.multiple_of(x * BY, BY), BY)
            E[f, to, :] = E[f, to, :] + total

        exchange(late_pred[1], late_pred[0], "wait_recv")
        planes(4, BX + 2, 2, second_lamb)
        deposit(LC, True, more_source)
        for c in (a2_left_p, a2_right_p, a2_left, a2_right):
            c.wait_recv()

        def correct(x):
            tend = rate_x(state_p, x)
            at = pl.ds(pl.multiple_of((x + H) * BY, BY), BY)
            to = pl.ds(pl.multiple_of(x * BY, BY), BY)
            for f in range(4):
                t = tend[f] - E[f - 1, to, :] if f else tend[f]
                final[f, to, :] = 0.5 * (
                    state[f, at, :] + state_p[f, at, :] + ape_time_step * t
                )

        planes(0, BX, 2, correct)
        for c in tables + relays + [a1_left, a1_right, a2_left, a2_right]:
            c.wait_send()
        for c in (a2_left_p, a2_right_p):
            c.wait_send()
        for pair in (edge_own_1, edge_own_2, edge_prev_1, edge_prev_2, edge_pred, late_pred):
            exchange(*pair, "wait_send")
        for lows, highs in ((a1_low, a1_high), (a2_low, a2_high)):
            for low, high in zip(lows, highs):
                exchange(low, high, "wait_send")


def on_device(flow_state, block_offset, block_weight):
    gx_size, gy_size = lax.axis_size("gx"), lax.axis_size("gy")

    def vmem(*shape):
        return pltpu.VMEM(shape, f32)

    def planes_of(fields, count):
        return vmem(fields, count * BY, NZ)

    scratch = [
        planes_of(4, BX + 2),
        *[vmem(4, BX, NZ)] * 4,
        planes_of(4, BX + 2),
        *[vmem(4, BX, NZ)] * 4,
        planes_of(4, BX + 2 * H),
        vmem(2, BX, 3 * BY, NZ),
        planes_of(3, 3 * BX),
        *[vmem(3, 3 * BX, NZ)] * 2,
        *[vmem(3, 2 * BX, NZ)] * 2,
        planes_of(3, 3 * BX),
        *[vmem(3, 3 * BX, NZ)] * 4,
        planes_of(3, 3 * BX),
        planes_of(3, 3 * BX),
        planes_of(4, BX),
        planes_of(4, BX + 2 * H),
        vmem(2, BX, 3 * BY, NZ),
        planes_of(3, BX),
        planes_of(3, BX),
        vmem(3, BY, NZ),
        vmem(25, BY, NZ),
        pltpu.SMEM((NB,), jnp.int32),
        pltpu.SMEM((NB,), f32),
        pltpu.SemaphoreType.DMA((N_REMOTE,)),
        pltpu.SemaphoreType.DMA((N_REMOTE,)),
        pltpu.SemaphoreType.DMA((N_LOCAL,)),
    ]
    anywhere = pl.BlockSpec(memory_space=pltpu.HBM)
    advanced = pl.pallas_call(
        functools.partial(kernel, gx_size, gy_size),
        out_shape=jax.ShapeDtypeStruct((4, BX * BY, NZ), f32),
        in_specs=[anywhere] * 4,
        out_specs=pl.BlockSpec(memory_space=pltpu.VMEM),
        scratch_shapes=scratch,
        compiler_params=pltpu.CompilerParams(collective_id=0, has_side_effects=True, vmem_limit_bytes=56250000),
        name="heun",
    )(flow_state.reshape(4, BX * BY, NZ), flow_state[0], block_offset, block_weight)
    return advanced.reshape(flow_state.shape)


def solution(mesh):
    placed = (P("grp", None, "gx", "gy", None), P("gx"), P("gx"))
    return jax.shard_map(
        on_device,
        mesh=mesh,
        in_specs=placed,
        out_specs=P("grp", None, "gx", "gy", None),
        check_vma=False,
    )
```

```python
import functools

import jax
import jax.numpy as jnp
from jax import lax
from jax.experimental import pallas as pl
from jax.experimental.pallas import tpu as pltpu
from jax.sharding import PartitionSpec as P

drp_weights = (
    0.907646591371,
    -0.337048393268,
    0.133442885327,
    -0.045246480208,
    0.011169294114,
    -0.001456501759,
)
viscosity = 0.05
mean_flow = 0.5
les_time_step = 0.1
ape_time_step = 0.4

MESH = pl.DeviceIdType.MESH
f32 = jnp.float32

BX = 16
BY = 8
NB = 4
BC = BX // NB
NZ = 128
H = 6

(
    LES_XL, LES_XR, LES_YL, LES_YH,
    PRED_XL, PRED_XR, PRED_YL, PRED_YH,
    RAW_0, RAW_1, RAW_2, RAW_NEXT,
    RELAY_0, RELAY_1, RELAY_2,
    TAB_L, TAB_R,
    A1_XL, A1_XR, A1_YLP, A1_YLV, A1_YHP, A1_YHV,
    A2_XL, A2_XR, A2_XLP, A2_XRP, A2_YLP, A2_YLV, A2_YHP, A2_YHV,
    EDGE_NEXT_L, EDGE_NEXT_H,
    OWN_1_L, OWN_1_H, OWN_2_L, OWN_2_H, PREV_1_L, PREV_1_H, PREV_2_L, PREV_2_H,
    EDGE_P_L, EDGE_P_H, LATE_P_L, LATE_P_H,
    N_REMOTE,
) = range(46)
L_FLOW, L_YP, L_YV, L_OFF, L_WT, L_OUT, N_LOCAL = range(7)


def sublane():
    return lax.broadcasted_iota(jnp.int32, (BY, NZ), 0)


def cells_of(first, count):
    return pl.ds(first * BY, count * BY)


def row(ref, f, p):
    return jnp.broadcast_to(ref[f, pl.ds(p, 1), :], (BY, NZ))


def around(cells, low, high, f, plane, edge):
    base = pl.multiple_of(plane * BY, BY)
    centre = cells[f, pl.ds(base, BY), :]
    x_m = cells[f, pl.ds(base - BY, BY), :]
    x_p = cells[f, pl.ds(base + BY, BY), :]
    sub = sublane()
    y_m = jnp.where(sub == 0, row(low, f, edge), pltpu.roll(centre, 1, 0))
    y_p = jnp.where(sub == BY - 1, row(high, f, edge), pltpu.roll(centre, BY - 1, 0))
    z_m = pltpu.roll(centre, 1, 1)
    z_p = pltpu.roll(centre, NZ - 1, 1)
    return centre, x_m, x_p, y_m, y_p, z_m, z_p


def lamb_of(near):
    grad = [
        [0.5 * (n[2] - n[1]), 0.5 * (n[4] - n[3]), 0.5 * (n[6] - n[5])] for n in near[:3]
    ]
    u, v, w = near[0][0], near[1][0], near[2][0]
    vort_x = grad[2][1] - grad[1][2]
    vort_y = grad[0][2] - grad[2][0]
    vort_z = grad[1][0] - grad[0][1]
    lamb = (vort_y * w - vort_z * v, vort_z * u - vort_x * w, vort_x * v - vort_y * u)
    return lamb


def spread_of(n):
    return -6.0 * n[0] + n[2] + n[1] + n[4] + n[3] + n[6] + n[5]


def les_tendency(near):
    lamb = lamb_of(near)
    tend = [-lamb[f] + viscosity * spread_of(near[f]) for f in range(3)]
    if len(near) == 4:
        n = near[3]
        carried = (
            near[0][0] * (0.5 * (n[2] - n[1]))
            + near[1][0] * (0.5 * (n[4] - n[3]))
            + near[2][0] * (0.5 * (n[6] - n[5]))
        )
        tend.append(-carried + viscosity * spread_of(n))
    return tend, lamb


def planes(first, last, unroll, body):
    count = last - first
    assert count % unroll == 0

    def step(i, carry):
        for k in range(unroll):
            body(first + i * unroll + k)
        return carry

    lax.fori_loop(0, count // unroll, step, 0)


def kernel(
    gx_size, gy_size,
    flow, flow_planes, offset, weight, out,
    X, XL, XH, EL, EH, XP, PL, PH, QL, QH,
    F, YE, R, RL, RH, SL, SH, V, VL, VH, WL, WH, LB, LC, G, FP, YP, D, E, TAB, COEF,
    off_s, wt_s, send_sem, recv_sem, local_sem,
):
    grp, gx, gy = lax.axis_index("grp"), lax.axis_index("gx"), lax.axis_index("gy")
    right = lax.rem(gx + 1, gx_size)
    left = lax.rem(gx + gx_size - 1, gx_size)
    has_low, has_high = gy > 0, gy < gy_size - 1
    is_les, is_ape = grp == 0, grp == 1
    place = lax.rem(gx, 4)

    def copy(kind, src, dst, device):
        return pltpu.make_async_remote_copy(
            src_ref=src,
            dst_ref=dst,
            send_sem=send_sem.at[kind],
            recv_sem=recv_sem.at[kind],
            device_id=device,
            device_id_type=MESH,
        )

    def here(kind, src, dst):
        return pltpu.make_async_copy(src, dst, local_sem.at[kind])

    me_left, me_right = (grp, left, gy), (grp, right, gy)
    me_low, me_high = (grp, gx, gy - 1), (grp, gx, gy + 1)

    les_first = [
        copy(LES_XL, flow.at[:, cells_of(0, 1)], X.at[:, cells_of(BX + 1, 1)], me_left),
        copy(LES_XR, flow.at[:, cells_of(BX - 1, 1)], X.at[:, cells_of(0, 1)], me_right),
    ]
    pieces = [(8, 8), (3, 5), (0, 3)]
    velocity = pl.ds(0, 3)
    les_raw = [
        copy(
            RAW_0 + k,
            flow.at[velocity, cells_of(first, count)],
            R.at[:, cells_of(BX + first, count)],
            (1, gx, gy),
        )
        for k, (first, count) in enumerate(pieces)
    ]
    les_next = copy(
        RAW_NEXT, flow.at[velocity, cells_of(0, 14)], R.at[:, cells_of(2 * BX, 14)], (1, left, gy)
    )
    les_edge_low = copy(LES_YL, EL, XH, me_low)
    les_edge_high = copy(LES_YH, EH, XL, me_high)
    pred_x = [
        copy(PRED_XL, XP.at[:, cells_of(1, 1)], XP.at[:, cells_of(BX + 1, 1)], me_left),
        copy(PRED_XR, XP.at[:, cells_of(BX, 1)], XP.at[:, cells_of(0, 1)], me_right),
    ]
    pred_low = copy(PRED_YL, QL, PH, me_low)
    pred_high = copy(PRED_YH, QH, PL, me_high)

    relays = []
    for k, (first, count) in enumerate(pieces):
        start = max(first, 2)
        count = first + count - start
        relays.append(
            copy(
                RELAY_0 + k,
                R.at[:, cells_of(BX + start, count)],
                R.at[:, cells_of(start, count)],
                me_right,
            )
        )
    tables = [
        copy(TAB_L, TAB.at[1], TAB.at[2], me_left),
        copy(TAB_R, TAB.at[1], TAB.at[0], me_right),
    ]
    a1_left = copy(A1_XL, flow.at[:, cells_of(0, H)], F.at[:, cells_of(BX + H, H)], me_left)
    a1_right = copy(A1_XR, flow.at[:, cells_of(BX - H, H)], F.at[:, cells_of(0, H)], me_right)
    low_part, own_part, high_part = pl.ds(0, BY), pl.ds(BY, BY), pl.ds(2 * BY, BY)
    a1_low = [
        copy(A1_YLP, flow_planes.at[0], YE.at[0, :, high_part], me_low),
        copy(A1_YLV, flow_planes.at[2], YE.at[1, :, high_part], me_low),
    ]
    a1_high = [
        copy(A1_YHP, flow_planes.at[0], YE.at[0, :, low_part], me_high),
        copy(A1_YHV, flow_planes.at[2], YE.at[1, :, low_part], me_high),
    ]
    own = cells_of(H, BX)
    flows = pl.ds(1, 3)
    a2_left = copy(A2_XL, FP.at[flows, cells_of(H, H)], FP.at[flows, cells_of(BX + H, H)], me_left)
    a2_right = copy(A2_XR, FP.at[flows, cells_of(BX, H)], FP.at[flows, cells_of(0, H)], me_right)
    a2_left_p = copy(A2_XLP, FP.at[0, cells_of(H, H)], FP.at[0, cells_of(BX + H, H)], me_left)
    a2_right_p = copy(A2_XRP, FP.at[0, cells_of(BX, H)], FP.at[0, cells_of(0, H)], me_right)
    a2_low = [
        copy(A2_YLP, YP.at[0, :, own_part], YP.at[0, :, high_part], me_low),
        copy(A2_YLV, YP.at[1, :, own_part], YP.at[1, :, high_part], me_low),
    ]
    a2_high = [
        copy(A2_YHP, YP.at[0, :, own_part], YP.at[0, :, low_part], me_high),
        copy(A2_YHV, YP.at[1, :, own_part], YP.at[1, :, low_part], me_high),
    ]
    third = [pl.ds(0, BX), pl.ds(BX, BX), pl.ds(2 * BX, BX)]

    edge_next = (
        copy(EDGE_NEXT_L, EL.at[velocity], RH.at[:, third[2]], (1, left, gy - 1)),
        copy(EDGE_NEXT_H, EH.at[velocity], RL.at[:, third[2]], (1, left, gy + 1)),
    )

    def edges(kind, first):
        part = pl.ds(first, 8)
        return (
            copy(kind, SL.at[:, part], RH.at[:, part], me_low),
            copy(kind + 1, SH.at[:, part], RL.at[:, part], me_high),
        )

    edge_own_1, edge_own_2 = edges(OWN_1_L, BX + 8), edges(OWN_2_L, BX)
    edge_prev_1, edge_prev_2 = edges(PREV_1_L, 8), edges(PREV_2_L, 0)
    soon, late = pl.ds(BX, 2 * BX), pl.ds(0, BX)
    edge_pred = (
        copy(EDGE_P_L, WL.at[:, soon], VH.at[:, soon], me_low),
        copy(EDGE_P_H, WH.at[:, soon], VL.at[:, soon], me_high),
    )
    late_pred = (
        copy(LATE_P_L, WL.at[:, late], VH.at[:, late], me_low),
        copy(LATE_P_H, WH.at[:, late], VL.at[:, late], me_high),
    )

    @pl.when(is_les)
    def _():
        here(L_FLOW, flow, X.at[:, cells_of(1, BX)]).start()

    @pl.when(is_ape)
    def _():
        here(L_FLOW, flow, F.at[:, own]).start()
        here(L_YP, flow_planes.at[0], YE.at[0, :, own_part]).start()
        here(L_YV, flow_planes.at[2], YE.at[1, :, own_part]).start()
        here(L_OFF, offset, off_s).start()
        here(L_WT, weight, wt_s).start()

    barrier = pltpu.get_barrier_semaphore()

    def greet(device):
        pl.semaphore_signal(barrier, inc=1, device_id=device, device_id_type=MESH)

    greet(me_left)
    greet(me_right)
    greet((1 - grp, gx, gy))

    @pl.when(is_les)
    def _():
        greet((1, left, gy))

        @pl.when(has_low)
        def _():
            greet((1, left, gy - 1))

        @pl.when(has_high)
        def _():
            greet((1, left, gy + 1))

    @pl.when(is_ape)
    def _():
        greet((0, right, gy))

        @pl.when(has_low)
        def _():
            greet((0, right, gy - 1))

        @pl.when(has_high)
        def _():
            greet((0, right, gy + 1))

    @pl.when(has_low)
    def _():
        greet(me_low)

    @pl.when(has_high)
    def _():
        greet(me_high)

    zeros_edge = jnp.zeros((48, NZ), f32)

    @pl.when(jnp.logical_not(has_low))
    def _():
        for f in range(4):
            XL[f] = zeros_edge[:BX]
            PL[f] = zeros_edge[:BX]
        for f in range(3):
            RL[f] = zeros_edge
            VL[f] = zeros_edge
        for f in range(2):
            YE[f, :, pl.ds(0, BY)] = jnp.zeros((BX, BY, NZ), f32)
            YP[f, :, pl.ds(0, BY)] = jnp.zeros((BX, BY, NZ), f32)

    @pl.when(jnp.logical_not(has_high))
    def _():
        for f in range(4):
            XH[f] = zeros_edge[:BX]
            PH[f] = zeros_edge[:BX]
        for f in range(3):
            RH[f] = zeros_edge
            VH[f] = zeros_edge
        for f in range(2):
            YE[f, :, pl.ds(2 * BY, BY)] = jnp.zeros((BX, BY, NZ), f32)
            YP[f, :, pl.ds(2 * BY, BY)] = jnp.zeros((BX, BY, NZ), f32)

    y_neighbours = jnp.where(has_low, 1, 0) + jnp.where(has_high, 1, 0)

    def exchange(low, high, what):
        @pl.when(has_low)
        def _():
            getattr(low, what)()

        @pl.when(has_high)
        def _():
            getattr(high, what)()

    def pack(cells, first, count, low, high, at, fields):
        for f in range(fields):
            low[f, pl.ds(at, count), :] = cells[f, pl.ds(first * BY, count, stride=BY), :]
            high[f, pl.ds(at, count), :] = cells[
                f, pl.ds(first * BY + BY - 1, count, stride=BY), :
            ]

    @pl.when(is_les)
    def les():
        cells, ahead, final = X, XP, out
        here(L_FLOW, flow, X.at[:, cells_of(1, BX)]).wait()
        pack(cells, 1, BX, EL, EH, 0, 4)
        pl.semaphore_wait(barrier, 4 + 2 * y_neighbours)
        exchange(*edge_next, "start")
        for c in les_raw[:2] + [les_next] + les_first + les_raw[2:]:
            c.start()
        exchange(les_edge_low, les_edge_high, "start")
        for c in les_first:
            c.wait_recv()
        exchange(les_edge_high, les_edge_low, "wait_recv")

        def predict(x):
            near = [around(cells, XL, XH, f, x + 1, x) for f in range(4)]
            tend, _ = les_tendency(near)
            for f in range(4):
                ahead[f, pl.ds(pl.multiple_of((x + 1) * BY, BY), BY), :] = (
                    near[f][0] + les_time_step * tend[f]
                )

        planes(0, BX, 2, predict)
        for c in pred_x:
            c.start()
        pack(ahead, 1, BX, QL, QH, 0, 4)
        exchange(pred_low, pred_high, "start")
        for c in pred_x:
            c.wait_recv()
        exchange(pred_high, pred_low, "wait_recv")

        def correct(x):
            near = [around(ahead, PL, PH, f, x + 1, x) for f in range(4)]
            tend, _ = les_tendency(near)
            for f in range(4):
                before = cells[f, pl.ds(pl.multiple_of((x + 1) * BY, BY), BY), :]
                final[f, pl.ds(pl.multiple_of(x * BY, BY), BY), :] = 0.5 * (
                    before + near[f][0] + les_time_step * tend[f]
                )

        planes(0, BX, 2, correct)
        for c in les_raw + [les_next] + les_first + pred_x:
            c.wait_send()
        exchange(les_edge_low, les_edge_high, "wait_send")
        exchange(pred_low, pred_high, "wait_send")
        exchange(*edge_next, "wait_send")

    @pl.when(is_ape)
    def ape():
        raw, state, ahead, rate, state_p, final = R, F, V, G, FP, out

        here(L_OFF, offset, off_s).wait()
        here(L_WT, weight, wt_s).wait()
        sub = sublane()
        table = jnp.zeros((BY, NZ), f32)
        for b in range(NB):
            table = jnp.where(sub == b, off_s[b].astype(f32), table)
            table = jnp.where(sub == NB + b, wt_s[b], table)
        TAB[1] = table

        pl.semaphore_wait(barrier, 4 + 2 * y_neighbours)
        for c in tables:
            c.start()

        @pl.when((place == 0))
        def _():
            a1_right.start()


        @pl.when((place == 1) | (place == 2) | (place == 3))
        def _():
            a1_left.start()

        for low, high in zip(a1_low, a1_high):
            exchange(low, high, "start")

        def thirteen(plus, minus):
            total = None
            for j, c in enumerate(drp_weights, start=1):
                term = c * (plus(j) - minus(j))
                total = term if total is None else total + term
            return total

        def rate_z(cells):
            def body(x):
                at = pl.multiple_of((x + H) * BY, BY)
                to = pl.ds(pl.multiple_of(x * BY, BY), BY)
                p, w = cells[0, pl.ds(at, BY), :], cells[3, pl.ds(at, BY), :]
                dz = [
                    thirteen(lambda j: pltpu.roll(q, NZ - j, 1), lambda j: pltpu.roll(q, j, 1))
                    for q in (p, w)
                ]
                rate[0, to, :] = -dz[1]
                rate[3, to, :] = -dz[0]

            planes(0, BX, 2, body)

        def rate_y(walls):
            def body(x):
                to = pl.ds(pl.multiple_of(x * BY, BY), BY)
                dy = [
                    thirteen(
                        lambda j: walls[f, x, pl.ds(BY + j, BY), :],
                        lambda j: walls[f, x, pl.ds(BY - j, BY), :],
                    )
                    for f in range(2)
                ]
                rate[0, to, :] = rate[0, to, :] - dy[1]
                rate[2, to, :] = -dy[0]

            planes(0, BX, 2, body)

        def rate_x(cells, x):
            at = (x + H) * BY

            def along(f):
                return thirteen(
                    lambda j: cells[f, pl.ds(pl.multiple_of(at + j * BY, BY), BY), :],
                    lambda j: cells[f, pl.ds(pl.multiple_of(at - j * BY, BY), BY), :],
                )

            to = pl.ds(pl.multiple_of(x * BY, BY), BY)
            dx = [along(f) for f in range(4)]
            return (
                rate[0, to, :] - mean_flow * dx[0] - dx[1],
                -mean_flow * dx[1] - dx[0],
                rate[2, to, :] - mean_flow * dx[2],
                rate[3, to, :] - mean_flow * dx[3],
            )

        here(L_FLOW, flow, F.at[:, own]).wait()
        rate_z(state)

        pairs = []
        for d in range(NB):
            for part, shift in enumerate((NB, 0, -NB)):
                for b in range(NB):
                    near_block, far_block = 1 - NB, NB
                    lowest = b + (near_block if b < NB - 1 else 0)
                    highest = b + (far_block if b > 0 else 0)
                    if lowest <= d + shift <= highest:
                        pairs.append((d, part, b, d + shift))

        def first_lamb(p):
            near = [around(raw, RL, RH, f, p, p) for f in range(3)]
            tend, lamb = les_tendency(near)
            to = pl.ds(pl.multiple_of(p * BY, BY), BY)
            for f in range(3):
                ahead[f, to, :] = near[f][0] + les_time_step * tend[f]
                LB[f, to, :] = lamb[f]

        def second_lamb(p):
            near = [around(ahead, VL, VH, f, p, p - 1) for f in range(3)]
            lamb = lamb_of(near)
            to = pl.ds(pl.multiple_of(p * BY, BY), BY)
            for f in range(3):
                LC[f, to, :] = lamb[f]

        def deposit(moved, is_late, add):
            for d in range(NB):
                terms = [
                    (k, part * BX + b * BC)
                    for k, (to, part, b, _) in enumerate(pairs)
                    if to == d and is_late == (part * NB + b <= NB)
                ]

                def body(r, carry):
                    for f in range(3):
                        total = None
                        for k, first in terms:
                            at = pl.multiple_of((first + r) * BY, BY)
                            term = COEF[k] * moved[f, pl.ds(at, BY), :]
                            total = term if total is None else total + term
                        add(f, d * BC + r, total)
                    return carry

                lax.fori_loop(0, BC, body, 0)

        def keep_in(ref):
            def add(f, x, total):
                ref[f, pl.ds(pl.multiple_of(x * BY, BY), BY), :] = total

            return add

        les_raw[0].wait_recv()
        les_raw[1].wait_recv()
        relays[0].start()
        relays[1].start()

        @pl.when((place == 0))
        def _():
            a1_left.start()


        @pl.when((place == 1) | (place == 3))
        def _():
            a1_right.start()

        pack(raw, BX + 8, 8, SL, SH, BX + 8, 3)
        exchange(*edge_own_1, "start")
        les_raw[2].wait_recv()
        relays[2].start()
        pack(raw, BX, 8, SL, SH, BX, 3)
        exchange(*edge_own_2, "start")

        exchange(edge_next[1], edge_next[0], "wait_recv")
        les_next.wait_recv()

        @pl.when((place == 2))
        def _():
            a1_right.start()

        exchange(edge_own_1[1], edge_own_1[0], "wait_recv")
        planes(BX + 9, 2 * BX + 13, 2, first_lamb)
        for c in tables:
            c.wait_recv()
        for k, (d, part, b, aim) in enumerate(pairs):
            target = row(TAB, part, b) + float(b)
            share = row(TAB, part, NB + b)
            COEF[k] = jnp.where(target == float(aim), share, 0.0) + jnp.where(
                target + 1.0 == float(aim), 1.0 - share, 0.0
            )

        here(L_YP, flow_planes.at[0], YE.at[0, :, own_part]).wait()
        here(L_YV, flow_planes.at[2], YE.at[1, :, own_part]).wait()
        for low, high in zip(a1_low, a1_high):
            exchange(high, low, "wait_recv")
        rate_y(YE)

        relays[0].wait_recv()
        pack(raw, 8, 8, SL, SH, 8, 3)
        exchange(*edge_prev_1, "start")
        relays[1].wait_recv()
        pack(raw, 3, 5, SL, SH, 3, 3)
        exchange(*edge_prev_2, "start")

        exchange(edge_own_2[1], edge_own_2[0], "wait_recv")
        planes(BX + 1, BX + 9, 4, first_lamb)
        pack(ahead, BX + 1, 28, WL, WH, BX, 3)
        exchange(*edge_pred, "start")
        deposit(LB, False, keep_in(D))

        a1_left.wait_recv()
        a1_right.wait_recv()

        def predict(x):
            tend = rate_x(state, x)
            at = pl.ds(pl.multiple_of((x + H) * BY, BY), BY)
            to = pl.ds(pl.multiple_of(x * BY, BY), BY)
            for f in range(4):
                t = tend[f] - D[f - 1, to, :] if f else tend[f]
                predicted = state[f, at, :] + ape_time_step * t
                state_p[f, at, :] = predicted
                if f == 0:
                    YP[0, x, own_part, :] = predicted

        planes(0, BX, 4, predict)
        a2_left_p.start()
        a2_right_p.start()
        exchange(a2_low[0], a2_high[0], "start")

        exchange(edge_prev_1[1], edge_prev_1[0], "wait_recv")
        planes(9, BX + 1, 4, first_lamb)
        exchange(edge_prev_2[1], edge_prev_2[0], "wait_recv")
        planes(4, 8, 4, first_lamb)
        planes(8, 9, 1, first_lamb)

        def take_source(f, x, total):
            at = pl.ds(pl.multiple_of((x + H) * BY, BY), BY)
            predicted = state_p[f + 1, at, :] - ape_time_step * total
            state_p[f + 1, at, :] = predicted
            if f == 1:
                YP[1, x, own_part, :] = predicted

        deposit(LB, True, take_source)
        a2_left.start()
        a2_right.start()
        exchange(a2_low[1], a2_high[1], "start")
        pack(ahead, 1, BX, WL, WH, 0, 3)
        exchange(*late_pred, "start")
        relays[2].wait_recv()
        planes(3, 4, 1, first_lamb)

        rate_z(state_p)
        exchange(edge_pred[1], edge_pred[0], "wait_recv")
        planes(BX + 2, BX + 28, 2, second_lamb)
        deposit(LC, False, keep_in(E))
        for low, high in zip(a2_low, a2_high):
            exchange(high, low, "wait_recv")
        rate_y(YP)

        def more_source(f, x, total):
            to = pl.ds(pl.multiple_of(x * BY, BY), BY)
            E[f, to, :] = E[f, to, :] + total

        exchange(late_pred[1], late_pred[0], "wait_recv")
        planes(4, BX + 2, 2, second_lamb)
        deposit(LC, True, more_source)
        for c in (a2_left_p, a2_right_p, a2_left, a2_right):
            c.wait_recv()

        def correct(x):
            tend = rate_x(state_p, x)
            at = pl.ds(pl.multiple_of((x + H) * BY, BY), BY)
            to = pl.ds(pl.multiple_of(x * BY, BY), BY)
            for f in range(4):
                t = tend[f] - E[f - 1, to, :] if f else tend[f]
                final[f, to, :] = 0.5 * (
                    state[f, at, :] + state_p[f, at, :] + ape_time_step * t
                )

        planes(0, BX, 4, correct)
        for c in tables + relays + [a1_left, a1_right, a2_left, a2_right]:
            c.wait_send()
        for c in (a2_left_p, a2_right_p):
            c.wait_send()
        for pair in (edge_own_1, edge_own_2, edge_prev_1, edge_prev_2, edge_pred, late_pred):
            exchange(*pair, "wait_send")
        for lows, highs in ((a1_low, a1_high), (a2_low, a2_high)):
            for low, high in zip(lows, highs):
                exchange(low, high, "wait_send")


def on_device(flow_state, block_offset, block_weight):
    gx_size, gy_size = lax.axis_size("gx"), lax.axis_size("gy")

    def vmem(*shape):
        return pltpu.VMEM(shape, f32)

    def planes_of(fields, count):
        return vmem(fields, count * BY, NZ)

    scratch = [
        planes_of(4, BX + 2),
        *[vmem(4, BX, NZ)] * 4,
        planes_of(4, BX + 2),
        *[vmem(4, BX, NZ)] * 4,
        planes_of(4, BX + 2 * H),
        vmem(2, BX, 3 * BY, NZ),
        planes_of(3, 3 * BX),
        *[vmem(3, 3 * BX, NZ)] * 2,
        *[vmem(3, 2 * BX, NZ)] * 2,
        planes_of(3, 3 * BX),
        *[vmem(3, 3 * BX, NZ)] * 4,
        planes_of(3, 3 * BX),
        planes_of(3, 3 * BX),
        planes_of(4, BX),
        planes_of(4, BX + 2 * H),
        vmem(2, BX, 3 * BY, NZ),
        planes_of(3, BX),
        planes_of(3, BX),
        vmem(3, BY, NZ),
        vmem(25, BY, NZ),
        pltpu.SMEM((NB,), jnp.int32),
        pltpu.SMEM((NB,), f32),
        pltpu.SemaphoreType.DMA((N_REMOTE,)),
        pltpu.SemaphoreType.DMA((N_REMOTE,)),
        pltpu.SemaphoreType.DMA((N_LOCAL,)),
    ]
    anywhere = pl.BlockSpec(memory_space=pltpu.HBM)
    advanced = pl.pallas_call(
        functools.partial(kernel, gx_size, gy_size),
        out_shape=jax.ShapeDtypeStruct((4, BX * BY, NZ), f32),
        in_specs=[anywhere] * 4,
        out_specs=pl.BlockSpec(memory_space=pltpu.VMEM),
        scratch_shapes=scratch,
        compiler_params=pltpu.CompilerParams(collective_id=0, has_side_effects=True, vmem_limit_bytes=56250000),
        name="heun",
    )(flow_state.reshape(4, BX * BY, NZ), flow_state[0], block_offset, block_weight)
    return advanced.reshape(flow_state.shape)


def solution(mesh):
    placed = (P("grp", None, "gx", "gy", None), P("gx"), P("gx"))
    return jax.shard_map(
        on_device,
        mesh=mesh,
        in_specs=placed,
        out_specs=P("grp", None, "gx", "gy", None),
        check_vma=False,
    )
```
